256 devices in a mesh: replica: 2 (over core), seq: 32 (over z, x), tensor: 4 (over y).
Axes of the slice: x: 4, y: 4, z: 8, core: 2. Of those that a mesh axis runs over, the one named last changes fastest.
Arguments:
- values: bfloat16 [2, 8192, 4096], P('replica', 'seq', 'tensor'), may hold values from -6 to 6
- gate_in: bfloat16 [2, 8192, 4096], P('replica', 'seq', 'tensor'), may hold values from -6 to 6
- in_b: bfloat16 [2, 8192, 128], P('replica', 'seq'), may hold values from -0.03125 to 0.03125
- in_c: bfloat16 [2, 8192, 128], P('replica', 'seq'), may hold values from -6 to 6
- step_sizes: float32 [2, 64, 8192], P('replica', 'tensor', 'seq'), may hold values from 0.2 to 8196
- log_rates: float32 [64], P('tensor'), as said below
- skip_gain: float32 [64], P('tensor'), may hold values from 0.5 to 1.5
- grad_out: bfloat16 [2, 8192, 4096], P('replica', 'seq', 'tensor'), may hold values from -6 to 6
Outputs:
- grad_values: bfloat16 [2, 8192, 4096], P('replica', 'seq', 'tensor')
- grad_gate: bfloat16 [2, 8192, 4096], P('replica', 'seq', 'tensor')
- grad_b: float32 [2, 8192, 128], P('replica', 'seq')
- grad_c: float32 [2, 8192, 128], P('replica', 'seq')
- grad_step_sizes: float32 [2, 64, 8192], P('replica', 'tensor', 'seq')
- grad_log_rates: float32 [64], P('tensor')
- derivative_bypass_weight: float32 [64], P('tensor')
The draws below stay inside these ranges and needn't reach their ends.
Inputs may be any that keep to these rules, and one draw needn't show every extreme that they name: `log_rates`: each entry is at least log(0.1 / 8192).
All inputs are finite; a program needn't handle non-finite values.
Results may differ from the reference program's by a relative error of at most 0.0047.
Values sent between devices are 32-bit elements; how exact they have to be, the bound alone decides.
A program may use at most 64 MiB of HBM per device.

```python
import math
import jax
import jax.numpy as jnp
from jax import lax

HEADS = 64
HEAD_DIM = 64
STATE = 128
TOK_DEV = 256
RUNS_IN_TOTAL = 2
TOKENS_PER_RUN = 8192


def draw_step_sizes(key, part):
    key_base = jax.random.fold_in(key, 11)
    key_factor = jax.random.fold_in(key, 12)
    key_spots = jax.random.fold_in(key, 13)
    random_seed_number = jax.random.fold_in(key, 14)
    baseline_steps = jax.random.uniform(key_base, (RUNS_IN_TOTAL, HEADS, TOKENS_PER_RUN), jnp.float32, 0.5, 1.5)
    block_count = TOKENS_PER_RUN // TOK_DEV
    rising = 3.0 ** (jnp.arange(block_count, dtype=jnp.float32) / max(block_count - 1, 1)) / math.sqrt(3.0)
    spike_factor = jax.random.uniform(key_factor, (RUNS_IN_TOTAL, HEADS, block_count), jnp.float32, 0.7, 1.4) * rising
    spike_factor = jnp.broadcast_to(spike_factor[:, :, :, None], (RUNS_IN_TOTAL, HEADS, block_count, TOK_DEV)).reshape(RUNS_IN_TOTAL, HEADS, TOKENS_PER_RUN)
    spike_positions = jax.random.randint(key_spots, (RUNS_IN_TOTAL, 3), 0, TOKENS_PER_RUN)
    outlier_indicator = jnp.any(jnp.arange(TOKENS_PER_RUN)[None, None, :] == spike_positions[:, :, None], axis=1)
    outlier_number = jax.random.uniform(random_seed_number, (RUNS_IN_TOTAL, TOKENS_PER_RUN), jnp.float32, 0.5, 1.0) * TOKENS_PER_RUN
    outlier_magnitudes = jnp.where(outlier_indicator, outlier_number, 0.0)
    return baseline_steps * spike_factor + outlier_magnitudes[:, None, :]


def draw_log_rates(key, part):
    key_pick = jax.random.fold_in(key, 21)
    key_slow = jax.random.fold_in(key, 22)
    key_fast = jax.random.fold_in(key, 23)
    share = 0.5
    slow_pick = jax.random.uniform(key_pick, (HEADS,), jnp.float32) < share
    slow_rate = jax.random.uniform(key_slow, (HEADS,), jnp.float32, 0.1, 0.5) / TOKENS_PER_RUN
    fast_rate = jnp.exp(jax.random.uniform(key_fast, (HEADS,), jnp.float32, math.log(0.02), math.log(0.06)))
    return jnp.log(jnp.where(slow_pick, slow_rate, fast_rate))


def block_scale(own_key, shape, shards, low, top_value):
    gain = 1.0
    for position, parts in shards:
        heights = jax.random.uniform(jax.random.fold_in(jax.random.fold_in(own_key, 6), position), (parts,), jnp.float32, low / len(shards), top_value / len(shards))
        gain = gain * jnp.repeat(jnp.exp(heights), shape[position] // parts).reshape((-1,) + (1,) * (len(shape) - 1 - position))
    return gain


def noise(own_key, shape, scale, most, cuts=(), held_as=jnp.bfloat16):
    array = scale * jax.random.normal(own_key, shape, jnp.float32)
    if cuts:
        array = array * block_scale(own_key, shape, cuts, -0.22, 0.18)
    return jnp.clip(array, -most, most).astype(held_as)


def setup_inputs(seed: int = 0) -> dict:
    arg_keys = jax.random.split(jax.random.key(seed), 9)
    return {
        "values": noise(arg_keys[0], (RUNS_IN_TOTAL, TOKENS_PER_RUN, HEADS * HEAD_DIM), 1.0, 6.0, ((0, 2), (1, 32), (2, 4))),
        "gate_in": noise(arg_keys[1], (RUNS_IN_TOTAL, TOKENS_PER_RUN, HEADS * HEAD_DIM), 1.0, 6.0, ((0, 2), (1, 32), (2, 4))),
        "in_b": noise(arg_keys[2], (RUNS_IN_TOTAL, TOKENS_PER_RUN, STATE), (STATE * TOK_DEV) ** -0.5, 0.03125, ((0, 2), (1, 32))),
        "in_c": noise(arg_keys[3], (RUNS_IN_TOTAL, TOKENS_PER_RUN, STATE), 1.0, 6.0, ((0, 2), (1, 32))),
        "step_sizes": draw_step_sizes(jax.random.fold_in(arg_keys[8], 71), 0),
        "log_rates": draw_log_rates(jax.random.fold_in(arg_keys[8], 71), 0),
        "skip_gain": jnp.clip(0.5 + 1.0 * jax.random.uniform(arg_keys[6], (HEADS,), jnp.float32) ** block_scale(arg_keys[6], (HEADS,), ((0, 4),), -0.2, 0.2), 0.5, 1.5),
        "grad_out": noise(arg_keys[7], (RUNS_IN_TOTAL, TOKENS_PER_RUN, HEADS * HEAD_DIM), 1.0, 6.0, ((0, 2), (1, 32), (2, 4))),
    }


def spread(per_head, head_width):
    head_count, length = per_head.shape
    return jnp.broadcast_to(per_head.T[:, :, None], (length, head_count, head_width)).reshape(length, head_count * head_width)


def head_sums(wide_rows, head_count):
    length = wide_rows.shape[0]
    return jnp.sum(wide_rows.reshape(length, head_count, -1), axis=2).T


def causal_decay(head_cum):
    length = head_cum.shape[0]
    row_ids = lax.broadcasted_iota(jnp.int32, (length, length), 0)
    col_ids = lax.broadcasted_iota(jnp.int32, (length, length), 1)
    causal = row_ids >= col_ids
    return jnp.where(causal, jnp.exp(jnp.where(causal, head_cum[:, None] - head_cum[None, :], 0.0)), 0.0)


def local_forward(block_vals, block_b, block_c, block_steps, decay_rates):
    head_count = block_steps.shape[0]
    head_width = block_vals.shape[1] // head_count
    logdecay = -decay_rates[:, None] * block_steps
    cumulative = jnp.cumsum(logdecay, axis=1)
    block_total = cumulative[:, -1]
    scores = jnp.dot(block_c, block_b.T, preferred_element_type=jnp.float32)

    def head_forward(head_index, intra_out):
        decay_mask = causal_decay(cumulative[head_index])
        mixing = (scores * decay_mask).astype(jnp.bfloat16)
        head_vals = lax.dynamic_slice_in_dim(block_vals, head_index * head_width, head_width, 1)
        piece_out = jnp.dot(mixing, head_vals, preferred_element_type=jnp.float32)
        return lax.dynamic_update_slice_in_dim(intra_out, piece_out, head_index * head_width, 1)

    intra_out = lax.fori_loop(0, head_count, head_forward, jnp.zeros(block_vals.shape, jnp.float32))
    scaled_exact = spread(jnp.exp(block_total[:, None] - cumulative), head_width) * block_vals
    scaled = scaled_exact.astype(jnp.bfloat16)
    device_hidden_memory = jnp.dot(scaled.T, block_b, preferred_element_type=jnp.float32).reshape(head_count, head_width, -1)
    return cumulative, block_total, scores, intra_out, scaled_exact, scaled, device_hidden_memory


def local_pull(block_c, block_gate, block_grad, cumulative, head_width):
    head_count = cumulative.shape[0]
    gate_wide = block_gate.astype(jnp.float32)
    gate_sigmoid = jax.nn.sigmoid(gate_wide)
    grad_y = block_grad.astype(jnp.float32) * (gate_wide * gate_sigmoid)
    growth = spread(jnp.exp(cumulative), head_width)
    grad_inter = growth * grad_y
    pulled = jnp.dot(grad_inter.T, block_c.astype(jnp.float32), precision=lax.Precision.HIGHEST)
    return gate_wide, gate_sigmoid, grad_y, growth, grad_inter, pulled.reshape(head_count, head_width, -1)


def local_rest(block_vals, block_b, block_c, block_grad, block_steps, decay_rates, skip_gain, forward_parts, pull_parts, entering, after):
    cumulative, block_total, scores, intra_out, scaled_exact, scaled, device_hidden_memory = forward_parts
    gate_wide, gate_sigmoid, grad_y, growth, grad_inter, pulled = pull_parts
    head_count, length = block_steps.shape
    head_width = block_vals.shape[1] // head_count
    entering_flat = entering.reshape(head_count * head_width, -1)
    after_flat = after.reshape(head_count * head_width, -1)
    inter_part = jnp.dot(block_c.astype(jnp.float32), entering_flat.T, precision=lax.Precision.HIGHEST)
    skip_wide = spread(jnp.broadcast_to(skip_gain[:, None], (head_count, length)), head_width)
    mamba_out = intra_out + growth * inter_part + skip_wide * block_vals
    grad_gate = (block_grad.astype(jnp.float32) * mamba_out * gate_sigmoid * (1.0 + gate_wide * (1.0 - gate_sigmoid))).astype(jnp.bfloat16)
    grad_y_b = grad_y.astype(jnp.bfloat16)

    def head_backward(head_index, carried):
        grad_inner, intra_cum, sum_c, sum_b = carried
        decay_mask = causal_decay(cumulative[head_index])
        mix_exact = scores * decay_mask
        mixing = mix_exact.astype(jnp.bfloat16)
        head_vals = lax.dynamic_slice_in_dim(block_vals, head_index * head_width, head_width, 1)
        head_grad = lax.dynamic_slice_in_dim(grad_y_b, head_index * head_width, head_width, 1)
        grad_mixing = jnp.dot(head_grad, head_vals.T, preferred_element_type=jnp.float32)
        grad_scores = (grad_mixing * decay_mask).astype(jnp.bfloat16)
        weighted = grad_mixing * mix_exact
        piece_grad = jnp.dot(mixing.T, head_grad, preferred_element_type=jnp.float32)
        grad_inner = lax.dynamic_update_slice_in_dim(grad_inner, piece_grad, head_index * head_width, 1)
        cum_row = jnp.sum(weighted, axis=1) - jnp.sum(weighted, axis=0)
        intra_cum = lax.dynamic_update_slice_in_dim(intra_cum, cum_row[None, :], head_index, 0)
        sum_c = sum_c + jnp.dot(grad_scores, block_b, preferred_element_type=jnp.float32)
        sum_b = sum_b + jnp.dot(grad_scores.T, block_c, preferred_element_type=jnp.float32)
        return grad_inner, intra_cum, sum_c, sum_b

    state_zeros = jnp.zeros(block_b.shape, jnp.float32)
    start = (jnp.zeros(block_vals.shape, jnp.float32), jnp.zeros((head_count, length), jnp.float32), state_zeros, state_zeros)
    grad_inner, intra_cum, sum_c, sum_b = lax.fori_loop(0, head_count, head_backward, start)
    grad_scaled = jnp.dot(block_b.astype(jnp.float32), after_flat.T, precision=lax.Precision.HIGHEST)
    out_decay = spread(jnp.exp(block_total[:, None] - cumulative), head_width)
    grad_values = (grad_inner + out_decay * grad_scaled + skip_wide * grad_y).astype(jnp.bfloat16)
    grad_c = sum_c + jnp.dot(grad_inter, entering_flat, precision=lax.Precision.HIGHEST)
    grad_b = sum_b + jnp.dot(scaled.astype(jnp.float32), after_flat, precision=lax.Precision.HIGHEST)
    from_inter = head_sums(grad_y * growth * inter_part, head_count)
    from_scaled = head_sums(grad_scaled * scaled_exact, head_count)
    grad_total = jnp.sum(from_scaled, axis=1) + jnp.exp(block_total) * jnp.sum(after * entering, axis=(1, 2))
    last_token = lax.broadcasted_iota(jnp.int32, (head_count, length), 1) == length - 1
    grad_cum = intra_cum + from_inter - from_scaled + jnp.where(last_token, grad_total[:, None], 0.0)
    grad_log = jnp.flip(jnp.cumsum(jnp.flip(grad_cum, axis=1), axis=1), axis=1)
    grad_steps = -decay_rates[:, None] * grad_log
    rate_part = -decay_rates * jnp.sum(block_steps * grad_log, axis=1)
    skip_part = jnp.sum(head_sums(grad_y * block_vals, head_count), axis=1)
    return grad_values, grad_gate, grad_b, grad_c, grad_steps, rate_part, skip_part


def reference(values, gate_in, in_b, in_c, step_sizes, log_rates, skip_gain, grad_out):
    block_count = TOKENS_PER_RUN // TOK_DEV
    decay_rates = jnp.exp(log_rates)
    collected = []
    for sequence in range(RUNS_IN_TOTAL):
        value_blocks = values[sequence].reshape(block_count, TOK_DEV, -1)
        gate_blocks = gate_in[sequence].reshape(block_count, TOK_DEV, -1)
        grad_blocks = grad_out[sequence].reshape(block_count, TOK_DEV, -1)
        b_blocks = in_b[sequence].reshape(block_count, TOK_DEV, STATE)
        c_blocks = in_c[sequence].reshape(block_count, TOK_DEV, STATE)
        step_blocks = step_sizes[sequence].reshape(HEADS, block_count, TOK_DEV).transpose(1, 0, 2)

        def first_section(pieces):
            block_vals, block_b, block_c, block_steps, block_gate, block_grad = pieces
            forward_parts = local_forward(block_vals, block_b, block_c, block_steps, decay_rates)
            pull_parts = local_pull(block_c, block_gate, block_grad, forward_parts[0], HEAD_DIM)
            return forward_parts[1], forward_parts[6], pull_parts[5]

        totals, local_states, pulls = lax.map(first_section, (value_blocks, b_blocks, c_blocks, step_blocks, gate_blocks, grad_blocks))

        def forward_link(carried, pieces):
            block_total, block_state = pieces
            return jnp.exp(block_total)[:, None, None] * carried + block_state, carried

        def backward_link(carried, pieces):
            block_total, block_pull = pieces
            return block_pull + jnp.exp(block_total)[:, None, None] * carried, carried

        state_zeros = jnp.zeros((HEADS, HEAD_DIM, STATE), jnp.float32)
        ignored, entering = lax.scan(forward_link, state_zeros, (totals, local_states))
        ignored, after = lax.scan(backward_link, state_zeros, (totals, pulls), reverse=True)

        def last_section(pieces):
            block_vals, block_b, block_c, block_steps, block_gate, block_grad, block_enter, block_after = pieces
            forward_parts = local_forward(block_vals, block_b, block_c, block_steps, decay_rates)
            pull_parts = local_pull(block_c, block_gate, block_grad, forward_parts[0], HEAD_DIM)
            return local_rest(block_vals, block_b, block_c, block_grad, block_steps, decay_rates, skip_gain, forward_parts, pull_parts, block_enter, block_after)

        block_results = lax.map(last_section, (value_blocks, b_blocks, c_blocks, step_blocks, gate_blocks, grad_blocks, entering, after))
        collected.append((
            block_results[0].reshape(TOKENS_PER_RUN, -1),
            block_results[1].reshape(TOKENS_PER_RUN, -1),
            block_results[2].reshape(TOKENS_PER_RUN, STATE),
            block_results[3].reshape(TOKENS_PER_RUN, STATE),
            block_results[4].transpose(1, 0, 2).reshape(HEADS, TOKENS_PER_RUN),
            jnp.sum(block_results[5], axis=0),
            jnp.sum(block_results[6], axis=0),
        ))
    grad_values = jnp.stack([entry[0] for entry in collected])
    grad_gate = jnp.stack([entry[1] for entry in collected])
    grad_b = jnp.stack([entry[2] for entry in collected])
    grad_c = jnp.stack([entry[3] for entry in collected])
    grad_step_sizes = jnp.stack([entry[4] for entry in collected])
    grad_log_rates = jnp.sum(jnp.stack([entry[5] for entry in collected]), axis=0)
    derivative_bypass_weight = jnp.sum(jnp.stack([entry[6] for entry in collected]), axis=0)
    return (grad_values, grad_gate, grad_b, grad_c, grad_step_sizes, grad_log_rates, derivative_bypass_weight)
```

```python
import functools

import jax
import jax.numpy as jnp
from jax import lax
from jax.experimental import pallas as pl
from jax.experimental.pallas import tpu as pltpu
from jax.sharding import PartitionSpec as P

F32 = jnp.float32
BF16 = jnp.bfloat16
NX, NZ, NY, NR = 4, 8, 4, 2
HEADS, HEAD, STATE, TOK = 16, 64, 128, 256
WIDE = HEADS * HEAD
SL = WIDE // NX
ZR = STATE // NZ
NT = (((1,), (1,)), ((), ()))
TN = (((0,), (0,)), ((), ()))
NN = (((1,), (0,)), ((), ()))


def mm(a, b, dims):
    return lax.dot_general(a, b, dims, preferred_element_type=F32)


def split2(x):
    hi = x.astype(BF16)
    return hi, (x - hi.astype(F32)).astype(BF16)


def split3(x):
    hi = x.astype(BF16)
    rest = x - hi.astype(F32)
    mid = rest.astype(BF16)
    return hi, mid, (rest - mid.astype(F32)).astype(BF16)


def iota(shape, dim):
    return lax.broadcasted_iota(jnp.int32, shape, dim)


def column(row):
    n = row.shape[1]
    same = iota((n, n), 0) == iota((n, n), 1)
    return jnp.sum(jnp.where(same, jnp.broadcast_to(row, (n, n)), 0.0), axis=1, keepdims=True)


def lanes_cumsum(x, reverse):
    n = x.shape[1]
    lane = iota(x.shape, 1)
    by = 1
    while by < n:
        if reverse:
            x = x + jnp.where(lane < n - by, pltpu.roll(x, n - by, 1), 0.0)
        else:
            x = x + jnp.where(lane >= by, pltpu.roll(x, by, 1), 0.0)
        by *= 2
    return x


def head_rows(rows, width):
    shape = (rows, rows * width)
    start = iota(shape, 0) * width
    lane = iota(shape, 1)
    return (lane >= start) & (lane < start + width)


def kernel(
    v_ref, g_ref, b_ref, c_ref, st_ref, lr_ref, sg_ref, go_ref,
    gv_ref, gg_ref, gb_ref, gc_ref, gs_ref, small_ref,
    cum_ref, cumcol_ref, grow_ref, decay_ref, skip_ref, scaled_ref, gy_ref, gyb_ref, gihi_ref, gilo_ref,
    gfac_ref, sc_ref, gsc_ref, intra_ref, inner_ref, w_ref, dw_ref, skipsum_ref,
    xs_ref, xr_ref, pre_ref, cs_ref, zs_ref, zr_ref, es_ref, er_ref, bs_ref, br_ref,
    ysum_ref, yr_ref, ya_ref, yg_ref, m1s_ref, m1_ref, m2s_ref, m2_ref,
    xs_sem, xr_sem, zs_sem, zr_sem, es_sem, er_sem, bs_sem, br_sem,
    ys_sem, yr_sem, as_sem, ar_sem, m1s_sem, m1r_sem, m2s_sem, m2r_sem,
):
    r = lax.axis_index("replica")
    seq = lax.axis_index("seq")
    y = lax.axis_index("tensor")
    z, x = seq // NX, seq % NX

    barrier = pltpu.get_barrier_semaphore()

    def at_x(to):
        return (r, z * NX + to, y)

    def at_z(to):
        return (r, to * NX + x, y)

    def at_y(to):
        return (r, seq, to)

    x_peers = [(x + o) % NX for o in (2, 1, 3)]
    z_peers = [(z + o) % NZ for o in (4, 3, 5, 2, 6, 1, 7)]
    y_peers = [(y + o) % NY for o in (2, 1, 3)]
    other = (r + 1) % NR
    met = [at_x(p) for p in x_peers] + [at_z(p) for p in z_peers] + [at_y(p) for p in y_peers]
    met += [(other, z * NX + p, y) for p in x_peers + [x]]
    for device in met:
        pl.semaphore_signal(barrier, inc=1, device_id=device, device_id_type=pl.DeviceIdType.MESH)

    def copy(src, dst, s, d, device):
        return pltpu.make_async_remote_copy(
            src_ref=src, dst_ref=dst, send_sem=s, recv_sem=d,
            device_id=device, device_id_type=pl.DeviceIdType.MESH,
        )

    rate = jnp.exp(column(lr_ref[...]))
    steps = st_ref[...]
    cum = lanes_cumsum(-rate * steps, False)
    total = cum[:, TOK - 1 : TOK]
    cum_ref[...] = cum
    marks = head_rows(HEADS, HEAD)
    marks_f = jnp.where(marks, 1.0, 0.0)
    marks_b = marks_f.astype(BF16)
    marks3 = jnp.concatenate([marks_b, marks_b, marks_b], axis=0)
    dw = jnp.sum(marks_f * jnp.exp(total), axis=0, keepdims=True)
    dw_ref[...] = dw
    skip_ref[...] = jnp.sum(marks_f * column(sg_ref[...]), axis=0, keepdims=True)
    for dst, what in ((decay_ref, jnp.exp(total - cum)), (grow_ref, jnp.exp(cum))):
        dst[...] = mm(jnp.concatenate(split3(what), axis=0), marks3, TN)

    b = b_ref[...]
    c = c_ref[...]

    def lanes(j):
        return pl.ds(pl.multiple_of(j * SL, SL), SL)

    def send_x(d, j, state):
        xs_ref[d, j, 0:STATE, :] = state
        xs_ref[d, j, STATE : STATE + 8, :] = jnp.broadcast_to(dw_ref[:, lanes(j)], (8, SL))

    def x_copy(d, j):
        return copy(xs_ref.at[d, j], xr_ref.at[d, x], xs_sem.at[d, j], xr_sem.at[d, x], at_x(j))

    for j in x_peers + [x]:
        at = lanes(j)
        scaled = (decay_ref[:, at] * v_ref[:, at].astype(F32)).astype(BF16)
        scaled_ref[:, at] = scaled
        send_x(0, j, mm(b, scaled, TN))
    xr_ref[0, x] = xs_ref[0, x]
    pl.semaphore_wait(barrier, len(met))
    for j in x_peers:
        x_copy(0, j).start()

    for j in x_peers + [x]:
        at = lanes(j)
        gate = g_ref[:, at].astype(F32)
        sig = 1.0 / (1.0 + jnp.exp(-gate))
        out = go_ref[:, at].astype(F32)
        gy = out * (gate * sig)
        gy_ref[:, at] = gy
        gyb_ref[:, at] = gy.astype(BF16)
        gfac_ref[:, at] = out * sig * (1.0 + gate * (1.0 - sig))
        hi, lo = split2(grow_ref[:, at] * gy)
        gihi_ref[:, at] = hi
        gilo_ref[:, at] = lo
        send_x(1, j, mm(c, hi, TN) + mm(c, lo, TN))
        skipsum_ref[:, at] = jnp.sum(gy * v_ref[:, at].astype(F32), axis=0, keepdims=True)
    xr_ref[1, x] = xs_ref[1, x]
    for j in x_peers:
        x_copy(1, j).start()

    sc_ref[...] = mm(c, b, NT)
    gsc_ref[...] = jnp.zeros_like(gsc_ref)
    wide = jnp.where(head_rows(HEADS, 128), 1.0, 0.0).astype(BF16)
    cumcol_ref[...] = mm(jnp.concatenate(split3(cum), axis=0), jnp.concatenate([wide] * 3, axis=0), TN)

    def pair(p, carried):
        at = pl.ds(pl.multiple_of(p * 128, 128), 128)
        vp, gp = v_ref[:, at], gyb_ref[:, at]
        lane = iota((TOK, 128), 1)
        causal = iota((128, 128), 0) >= iota((128, 128), 1)
        intra = jnp.zeros((TOK, 128), F32)
        inner = jnp.zeros((TOK, 128), F32)
        for k in range(2):
            h = p * 2 + k
            own = jnp.where(lane < HEAD, 1.0 - k, float(k)).astype(BF16)
            vm, gm = vp * own, gp * own
            col = cumcol_ref[:, pl.ds(pl.multiple_of(h * 128, 128), 128)]
            row = cum_ref[pl.ds(h, 1), :]
            d00 = jnp.where(causal, jnp.exp(col[:128] - row[:, :128]), 0.0)
            d10 = jnp.exp(col[128:] - row[:, :128])
            d11 = jnp.where(causal, jnp.exp(col[128:] - row[:, 128:]), 0.0)
            grad = mm(gm, vp, NT)
            gsc_ref[:128, :128] += grad[:128, :128] * d00
            gsc_ref[128:, :128] += grad[128:, :128] * d10
            gsc_ref[128:, 128:] += grad[128:, 128:] * d11
            m00 = (sc_ref[:128, :128] * d00).astype(BF16)
            m10 = (sc_ref[128:, :128] * d10).astype(BF16)
            m11 = (sc_ref[128:, 128:] * d11).astype(BF16)
            mix = jnp.concatenate(
                [jnp.concatenate([m00, jnp.zeros_like(m00)], axis=1), jnp.concatenate([m10, m11], axis=1)], axis=0
            )
            intra = intra + mm(mix, vm, NN)
            inner = inner + mm(mix, gm, TN)
        intra_ref[:, at] = intra
        inner_ref[:, at] = inner
        w_ref[:, at] = gp.astype(F32) * intra - vp.astype(F32) * inner
        return carried

    def pairs(first, last):
        lax.fori_loop(first, last, pair, 0)

    def x_level(d):
        for j in x_peers:
            copy(xs_ref.at[d, j], xr_ref.at[d, j], xs_sem.at[d, j], xr_sem.at[d, j], at_x(j)).wait_recv()
        order = range(NX) if d == 0 else range(NX - 1, -1, -1)
        state, through = jnp.zeros((STATE, SL), F32), jnp.ones((8, SL), F32)
        for i in order:
            pre_ref[d, i] = state
            cs_ref[d, i] = through
            decay = xr_ref[d, i, STATE : STATE + 8, :]
            state = decay[0:1] * state + xr_ref[d, i, 0:STATE, :]
            through = through * decay
        for i in range(NZ):
            zs_ref[d, i, 0:ZR, :] = state[i * ZR : (i + 1) * ZR]
            zs_ref[d, i, ZR : ZR + 8, :] = through
        zr_ref[d, z] = zs_ref[d, z]
        for i in z_peers:
            copy(zs_ref.at[d, i], zr_ref.at[d, z], zs_sem.at[d, i], zr_sem.at[d, z], at_z(i)).start()

    def z_level(d):
        for i in z_peers:
            copy(zs_ref.at[d, i], zr_ref.at[d, i], zs_sem.at[d, i], zr_sem.at[d, i], at_z(i)).wait_recv()
        order = range(NZ) if d == 0 else range(NZ - 1, -1, -1)
        state = jnp.zeros((ZR, SL), F32)
        for i in order:
            es_ref[d, i] = state
            state = zr_ref[d, i, ZR : ZR + 1, :] * state + zr_ref[d, i, 0:ZR, :]
        er_ref[d, z] = es_ref[d, z]
        for i in z_peers:
            copy(es_ref.at[d, i], er_ref.at[d, z], es_sem.at[d, i], er_sem.at[d, z], at_z(i)).start()

    def back(d):
        for i in z_peers:
            copy(es_ref.at[d, i], er_ref.at[d, i], es_sem.at[d, i], er_sem.at[d, i], at_z(i)).wait_recv()
        for j in x_peers + [x]:
            through = cs_ref[d, j, 0:1, :]
            for i in range(NZ):
                rows = slice(i * ZR, (i + 1) * ZR)
                bs_ref[d, j, rows, :] = pre_ref[d, j, rows, :] + through * er_ref[d, i]
        br_ref[d, x] = bs_ref[d, x]
        for j in x_peers:
            copy(bs_ref.at[d, j], br_ref.at[d, x], bs_sem.at[d, j], br_sem.at[d, x], at_x(j)).start()

    def arrived(d, j):
        copy(bs_ref.at[d, j], br_ref.at[d, j], bs_sem.at[d, j], br_sem.at[d, j], at_x(j)).wait_recv()

    def y_scatter(d, part):
        for q in range(NY):
            ysum_ref[d, q] = part[q * (TOK // NY) : (q + 1) * (TOK // NY)]
        yr_ref[d, y] = ysum_ref[d, y]
        for q in y_peers:
            copy(ysum_ref.at[d, q], yr_ref.at[d, y], ys_sem.at[d, q], yr_sem.at[d, y], at_y(q)).start()

    def y_gather(d):
        for q in y_peers:
            copy(ysum_ref.at[d, q], yr_ref.at[d, q], ys_sem.at[d, q], yr_sem.at[d, q], at_y(q)).wait_recv()
        ya_ref[d] = (yr_ref[d, 0] + yr_ref[d, 1]) + (yr_ref[d, 2] + yr_ref[d, 3])
        yg_ref[d, y] = ya_ref[d]
        for q in y_peers:
            copy(ya_ref.at[d], yg_ref.at[d, y], as_sem.at[d, q], ar_sem.at[d, y], at_y(q)).start()

    def y_finish(d, dst):
        for q in y_peers:
            copy(ya_ref.at[d], yg_ref.at[d, q], as_sem.at[d, q], ar_sem.at[d, q], at_y(q)).wait_recv()
        for q in range(NY):
            dst[q * (TOK // NY) : (q + 1) * (TOK // NY), :] = yg_ref[d, q]

    pairs(0, 2)
    x_level(0)
    pairs(2, 4)
    x_level(1)
    pairs(4, 6)
    z_level(0)
    pairs(6, 8)
    z_level(1)
    gsc_hi, gsc_lo = split2(gsc_ref[...])
    part_c = mm(gsc_hi, b, NN) + mm(gsc_lo, b, NN)
    part_b = mm(gsc_hi, c, TN) + mm(gsc_lo, c, TN)
    back(0)
    back(1)

    for n, j in enumerate([x] + x_peers[1:] + x_peers[:1]):
        if n:
            arrived(0, j)
        at = lanes(j)
        hi, lo = split2(br_ref[0, j])
        inter = mm(c, hi, NN) + mm(c, lo, NN)
        mamba = intra_ref[:, at] + grow_ref[:, at] * inter + skip_ref[:, at] * v_ref[:, at].astype(F32)
        gg_ref[:, at] = (gfac_ref[:, at] * mamba).astype(BF16)
        gi_hi, gi_lo = gihi_ref[:, at], gilo_ref[:, at]
        w_ref[:, at] += (gi_hi.astype(F32) + gi_lo.astype(F32)) * inter
        part_c = part_c + (mm(gi_hi, hi, NT) + mm(gi_lo, hi, NT) + mm(gi_hi, lo, NT))
    y_scatter(0, part_c)

    grad_cum = jnp.zeros((HEADS, TOK), F32)
    for n, j in enumerate([x] + x_peers[1:] + x_peers[:1]):
        if n:
            arrived(1, j)
        at = lanes(j)
        after = br_ref[1, j]
        hi, lo = split2(after)
        grad_scaled = mm(b, hi, NN) + mm(b, lo, NN)
        out_decay = decay_ref[:, at]
        gv_ref[:, at] = (inner_ref[:, at] + out_decay * grad_scaled + skip_ref[:, at] * gy_ref[:, at]).astype(BF16)
        from_scaled = grad_scaled * (out_decay * v_ref[:, at].astype(F32))
        last = jnp.sum(from_scaled, axis=0, keepdims=True)
        last = last + dw_ref[:, at] * jnp.sum(after * br_ref[0, j], axis=0, keepdims=True)
        w = w_ref[:, at] - from_scaled + jnp.where(iota((TOK, SL), 0) == TOK - 1, last, 0.0)
        start = iota((HEADS, SL), 0) * HEAD - j * SL
        lane = iota((HEADS, SL), 1)
        mark = jnp.where((lane >= start) & (lane < start + HEAD), 1.0, 0.0).astype(BF16)
        w_hi, w_mid, w_lo = split3(w)
        grad_cum = grad_cum + (mm(mark, w_hi, NT) + mm(mark, w_mid, NT) + mm(mark, w_lo, NT))
        scaled = scaled_ref[:, at]
        part_b = part_b + (mm(scaled, hi, NT) + mm(scaled, lo, NT))
    y_scatter(1, part_b)

    grad_log = lanes_cumsum(grad_cum, True)
    gs_ref[...] = -rate * grad_log
    rate_part = jnp.sum(-rate * steps * grad_log, axis=1, keepdims=True)
    skip_part = jnp.sum(jnp.where(marks, skipsum_ref[...], 0.0), axis=1, keepdims=True)
    own = r * NX + x
    m1s_ref[...] = jnp.where(iota((HEADS, 128), 1) < 64, rate_part, skip_part)
    m1_ref[own] = m1s_ref[...]
    near = [(r, p) for p in x_peers] + [(other, p) for p in x_peers + [x]]
    for rr, p in near:
        i = rr * NX + p
        copy(m1s_ref, m1_ref.at[own], m1s_sem.at[i], m1r_sem.at[own], (rr, z * NX + p, y)).start()
    y_gather(0)
    for rr, p in near:
        i = rr * NX + p
        copy(m1s_ref, m1_ref.at[i], m1s_sem.at[i], m1r_sem.at[i], (rr, z * NX + p, y)).wait_recv()
    m2s_ref[...] = ((m1_ref[0] + m1_ref[1]) + (m1_ref[2] + m1_ref[3])) + ((m1_ref[4] + m1_ref[5]) + (m1_ref[6] + m1_ref[7]))
    m2_ref[z] = m2s_ref[...]
    for i in z_peers:
        copy(m2s_ref, m2_ref.at[z], m2s_sem.at[i], m2r_sem.at[z], at_z(i)).start()
    y_gather(1)
    y_finish(0, gc_ref)
    y_finish(1, gb_ref)
    for i in z_peers:
        copy(m2s_ref, m2_ref.at[i], m2s_sem.at[i], m2r_sem.at[i], at_z(i)).wait_recv()
    small_ref[...] = ((m2_ref[0] + m2_ref[1]) + (m2_ref[2] + m2_ref[3])) + ((m2_ref[4] + m2_ref[5]) + (m2_ref[6] + m2_ref[7]))

    for d in range(2):
        for j in x_peers:
            x_copy(d, j).wait_send()
            copy(bs_ref.at[d, j], br_ref.at[d, x], bs_sem.at[d, j], br_sem.at[d, x], at_x(j)).wait_send()
        for i in z_peers:
            copy(zs_ref.at[d, i], zr_ref.at[d, z], zs_sem.at[d, i], zr_sem.at[d, z], at_z(i)).wait_send()
            copy(es_ref.at[d, i], er_ref.at[d, z], es_sem.at[d, i], er_sem.at[d, z], at_z(i)).wait_send()
        for q in y_peers:
            copy(ysum_ref.at[d, q], yr_ref.at[d, y], ys_sem.at[d, q], yr_sem.at[d, y], at_y(q)).wait_send()
            copy(ya_ref.at[d], yg_ref.at[d, y], as_sem.at[d, q], ar_sem.at[d, y], at_y(q)).wait_send()
    for rr, p in near:
        i = rr * NX + p
        copy(m1s_ref, m1_ref.at[own], m1s_sem.at[i], m1r_sem.at[own], (rr, z * NX + p, y)).wait_send()
    for i in z_peers:
        copy(m2s_ref, m2_ref.at[z], m2s_sem.at[i], m2r_sem.at[z], at_z(i)).wait_send()


def block(values, gate_in, in_b, in_c, step_sizes, log_rates, skip_gain, grad_out):
    vmem = pl.BlockSpec(memory_space=pltpu.VMEM)
    dma = pltpu.SemaphoreType.DMA
    scratch = [
        ((HEADS, TOK), F32), ((TOK, HEADS * 128), F32), ((TOK, WIDE), F32), ((TOK, WIDE), F32), ((1, WIDE), F32),
        ((TOK, WIDE), BF16), ((TOK, WIDE), F32), ((TOK, WIDE), BF16), ((TOK, WIDE), BF16), ((TOK, WIDE), BF16),
        ((TOK, WIDE), F32), ((TOK, TOK), F32), ((TOK, TOK), F32), ((TOK, WIDE), F32), ((TOK, WIDE), F32),
        ((TOK, WIDE), F32), ((1, WIDE), F32), ((1, WIDE), F32),
        ((2, NX, STATE + 8, SL), F32), ((2, NX, STATE + 8, SL), F32), ((2, NX, STATE, SL), F32), ((2, NX, 8, SL), F32),
        ((2, NZ, ZR + 8, SL), F32), ((2, NZ, ZR + 8, SL), F32), ((2, NZ, ZR, SL), F32), ((2, NZ, ZR, SL), F32),
        ((2, NX, STATE, SL), F32), ((2, NX, STATE, SL), F32),
        ((2, NY, TOK // NY, STATE), F32), ((2, NY, TOK // NY, STATE), F32), ((2, TOK // NY, STATE), F32),
        ((2, NY, TOK // NY, STATE), F32),
        ((HEADS, 128), F32), ((NX * NR, HEADS, 128), F32), ((HEADS, 128), F32), ((NZ, HEADS, 128), F32),
    ]
    sems = [(2, NX), (2, NX), (2, NZ), (2, NZ), (2, NZ), (2, NZ), (2, NX), (2, NX), (2, NY), (2, NY), (2, NY), (2, NY),
            (NX * NR,), (NX * NR,), (NZ,), (NZ,)]
    outs = [((TOK, WIDE), BF16), ((TOK, WIDE), BF16), ((TOK, STATE), F32), ((TOK, STATE), F32), ((HEADS, TOK), F32),
            ((HEADS, 128), F32)]
    gv, gg, gb, gc, gs, small = pl.pallas_call(
        kernel,
        out_shape=[jax.ShapeDtypeStruct(s, d) for s, d in outs],
        in_specs=[vmem] * 8,
        out_specs=[vmem] * 6,
        scratch_shapes=[pltpu.VMEM(s, d) for s, d in scratch] + [dma(s) for s in sems],
        compiler_params=pltpu.CompilerParams(collective_id=0, has_side_effects=True),
    )(values[0], gate_in[0], in_b[0], in_c[0], step_sizes[0], log_rates[None], skip_gain[None], grad_out[0])
    return gv[None], gg[None], gb[None], gc[None], gs[None], small[:, 0], small[:, 64]


def solution(mesh):
    wide = P("replica", "seq", "tensor")
    state = P("replica", "seq", None)
    step = P("replica", "tensor", "seq")
    head = P("tensor")
    return jax.shard_map(
        block,
        mesh=mesh,
        in_specs=(wide, wide, state, state, step, head, head, wide),
        out_specs=(wide, wide, state, state, step, head, head),
        check_vma=False,
    )
```

```python
import functools

import jax
import jax.numpy as jnp
from jax import lax
from jax.experimental import pallas as pl
from jax.experimental.pallas import tpu as pltpu
from jax.sharding import PartitionSpec as P

F32 = jnp.float32
BF16 = jnp.bfloat16
NX, NZ, NY, NR = 4, 8, 4, 2
HEADS, HEAD, STATE, TOK = 16, 64, 128, 256
WIDE = HEADS * HEAD
SL = WIDE // NX
PIECES = 2
CR = STATE // PIECES
ZR = CR // NZ
NT = (((1,), (1,)), ((), ()))
TN = (((0,), (0,)), ((), ()))
NN = (((1,), (0,)), ((), ()))


def mm(a, b, dims):
    return lax.dot_general(a, b, dims, preferred_element_type=F32)


def split2(x):
    hi = x.astype(BF16)
    return hi, (x - hi.astype(F32)).astype(BF16)


def split3(x):
    hi = x.astype(BF16)
    rest = x - hi.astype(F32)
    mid = rest.astype(BF16)
    return hi, mid, (rest - mid.astype(F32)).astype(BF16)


def iota(shape, dim):
    return lax.broadcasted_iota(jnp.int32, shape, dim)


def column(row):
    n = row.shape[1]
    same = iota((n, n), 0) == iota((n, n), 1)
    return jnp.sum(jnp.where(same, jnp.broadcast_to(row, (n, n)), 0.0), axis=1, keepdims=True)


def lanes_cumsum(x, reverse):
    n = x.shape[1]
    lane = iota(x.shape, 1)
    by = 1
    while by < n:
        if reverse:
            x = x + jnp.where(lane < n - by, pltpu.roll(x, n - by, 1), 0.0)
        else:
            x = x + jnp.where(lane >= by, pltpu.roll(x, by, 1), 0.0)
        by *= 2
    return x


def head_rows(rows, width):
    shape = (rows, rows * width)
    start = iota(shape, 0) * width
    lane = iota(shape, 1)
    return (lane >= start) & (lane < start + width)


def kernel(
    v_hbm, g_hbm, b_hbm, c_hbm, st_hbm, lr_hbm, sg_hbm, go_hbm,
    gv_ref, gg_ref, gb_ref, gc_ref, gs_ref, small_ref,
    v_ref, g_ref, b_ref, c_ref, st_ref, lr_ref, sg_ref, go_ref,
    cum_ref, cumcol_ref, grow_ref, decay_ref, skip_ref, scaled_ref, gy_ref, gyb_ref, gihi_ref, gilo_ref,
    gfac_ref, sc_ref, gsc_ref, intra_ref, inner_ref, w_ref, dw_ref, skipsum_ref,
    xd_ref, xdr_ref, cs_ref, zd_ref, zdr_ref,
    xs_ref, xr_ref, pre_ref, zs_ref, zr_ref, es_ref, er_ref, bs_ref, br_ref,
    ysum_ref, yr_ref, ya_ref, yg_ref, m1s_ref, m1_ref, m2s_ref, m2_ref,
    in_sem, xds_sem, xdr_sem, zds_sem, zdr_sem,
    xs_sem, xr_sem, zs_sem, zr_sem, es_sem, er_sem, bs_sem, br_sem,
    ys_sem, yr_sem, as_sem, ar_sem, m1s_sem, m1r_sem, m2s_sem, m2r_sem,
):
    r = lax.axis_index("replica")
    seq = lax.axis_index("seq")
    y = lax.axis_index("tensor")
    z, x = seq // NX, seq % NX

    barrier = pltpu.get_barrier_semaphore()

    def at_x(to):
        return (r, z * NX + to, y)

    def at_z(to):
        return (r, to * NX + x, y)

    def at_y(to):
        return (r, seq, to)

    x_peers = [(x + o) % NX for o in (2, 1, 3)]
    z_peers = [(z + o) % NZ for o in (4, 3, 5, 2, 6, 1, 7)]
    y_peers = [(y + o) % NY for o in (2, 1, 3)]
    other = (r + 1) % NR
    met = [at_z(p) for p in z_peers] + [at_x(p) for p in x_peers] + [at_y(p) for p in y_peers]
    met += [(other, z * NX + p, y) for p in x_peers + [x]]
    for device in met:
        pl.semaphore_signal(barrier, inc=1, device_id=device, device_id_type=pl.DeviceIdType.MESH)

    fetch = [
        pltpu.make_async_copy(src, dst, in_sem.at[i])
        for i, (src, dst) in enumerate((
            (lr_hbm, lr_ref), (sg_hbm, sg_ref), (st_hbm, st_ref), (b_hbm, b_ref),
            (v_hbm, v_ref), (c_hbm, c_ref), (g_hbm, g_ref), (go_hbm, go_ref),
        ))
    ]
    for f in fetch:
        f.start()

    def copy(src, dst, s, d, device):
        return pltpu.make_async_remote_copy(
            src_ref=src, dst_ref=dst, send_sem=s, recv_sem=d,
            device_id=device, device_id_type=pl.DeviceIdType.MESH,
        )

    for f in fetch[:3]:
        f.wait()
    rate = jnp.exp(column(lr_ref[...]))
    steps = st_ref[...]
    cum = lanes_cumsum(-rate * steps, False)
    total = cum[:, TOK - 1 : TOK]
    cum_ref[...] = cum
    marks = head_rows(HEADS, HEAD)
    marks_f = jnp.where(marks, 1.0, 0.0)
    marks_b = marks_f.astype(BF16)
    marks3 = jnp.concatenate([marks_b, marks_b, marks_b], axis=0)
    dw_ref[...] = jnp.sum(marks_f * jnp.exp(total), axis=0, keepdims=True)
    skip_ref[...] = jnp.sum(marks_f * column(sg_ref[...]), axis=0, keepdims=True)
    for dst, what in ((decay_ref, jnp.exp(total - cum)), (grow_ref, jnp.exp(cum))):
        dst[...] = mm(jnp.concatenate(split3(what), axis=0), marks3, TN)
    for j in range(NX):
        xd_ref[j] = jnp.broadcast_to(dw_ref[:, j * SL : (j + 1) * SL], (8, SL))
    xdr_ref[x] = xd_ref[x]

    for f in fetch[3:5]:
        f.wait()
    b = b_ref[...]

    def lanes(j):
        return pl.ds(pl.multiple_of(j * SL, SL), SL)

    def keep(d, j, state):
        for m in range(PIECES):
            xs_ref[d, m, j] = state[m * CR : (m + 1) * CR]

    def x_copy(d, m, j, i):
        return copy(xs_ref.at[d, m, j], xr_ref.at[d, m, i], xs_sem.at[d, m, j], xr_sem.at[d, m, i], at_x(j))

    def xd_copy(j, i):
        return copy(xd_ref.at[j], xdr_ref.at[i], xds_sem.at[j], xdr_sem.at[i], at_x(j))

    def zd_copy(j, i):
        return copy(zd_ref, zdr_ref.at[i], zds_sem.at[j], zdr_sem.at[i], at_z(j))

    def z_copy(d, m, j, i):
        return copy(zs_ref.at[d, m, j], zr_ref.at[d, m, i], zs_sem.at[d, m, j], zr_sem.at[d, m, i], at_z(j))

    def e_copy(d, m, j, i):
        return copy(es_ref.at[d, m, j], er_ref.at[d, m, i], es_sem.at[d, m, j], er_sem.at[d, m, i], at_z(j))

    def b_copy(d, m, j, i):
        return copy(
            bs_ref.at[d, m, j], br_ref.at[d, i, pl.ds(m * CR, CR)], bs_sem.at[d, m, j], br_sem.at[d, m, i], at_x(j)
        )

    for n, j in enumerate(x_peers + [x]):
        at = lanes(j)
        scaled = (decay_ref[:, at] * v_ref[:, at].astype(F32)).astype(BF16)
        scaled_ref[:, at] = scaled
        keep(0, j, mm(b, scaled, TN))
        if n == 0:
            pl.semaphore_wait(barrier, len(met))
            for i in x_peers:
                xd_copy(i, x).start()
        if n < NX - 1:
            x_copy(0, 0, j, x).start()
    for m in range(1, PIECES):
        for j in x_peers:
            x_copy(0, m, j, x).start()

    for f in fetch[5:]:
        f.wait()
    c = c_ref[...]
    for n, j in enumerate(x_peers + [x]):
        at = lanes(j)
        gate = g_ref[:, at].astype(F32)
        sig = 1.0 / (1.0 + jnp.exp(-gate))
        out = go_ref[:, at].astype(F32)
        gy = out * (gate * sig)
        gy_ref[:, at] = gy
        gyb_ref[:, at] = gy.astype(BF16)
        gfac_ref[:, at] = out * sig * (1.0 + gate * (1.0 - sig))
        hi, lo = split2(grow_ref[:, at] * gy)
        gihi_ref[:, at] = hi
        gilo_ref[:, at] = lo
        keep(1, j, mm(c, hi, TN) + mm(c, lo, TN))
        if n < NX - 1:
            x_copy(1, 0, j, x).start()
        skipsum_ref[:, at] = jnp.sum(gy * v_ref[:, at].astype(F32), axis=0, keepdims=True)
    for m in range(1, PIECES):
        for j in x_peers:
            x_copy(1, m, j, x).start()
    for d in range(2):
        for m in range(PIECES):
            xr_ref[d, m, x] = xs_ref[d, m, x]

    for j in x_peers:
        xd_copy(j, j).wait_recv()
    for d in range(2):
        through = jnp.ones((8, SL), F32)
        for i in range(NX) if d == 0 else range(NX - 1, -1, -1):
            cs_ref[d, i] = through
            through = through * xdr_ref[i]
        if d == 0:
            zd_ref[...] = through
    zdr_ref[z] = zd_ref[...]
    for i in z_peers:
        zd_copy(i, z).start()

    sc_ref[...] = mm(c, b, NT)
    gsc_ref[...] = jnp.zeros_like(gsc_ref)
    wide = jnp.where(head_rows(HEADS, 128), 1.0, 0.0).astype(BF16)
    cumcol_ref[...] = mm(jnp.concatenate(split3(cum), axis=0), jnp.concatenate([wide] * 3, axis=0), TN)

    def pair(p, carried):
        at = pl.ds(pl.multiple_of(p * 128, 128), 128)
        vp, gp = v_ref[:, at], gyb_ref[:, at]
        lane = iota((TOK, 128), 1)
        causal = iota((128, 128), 0) >= iota((128, 128), 1)
        intra = jnp.zeros((TOK, 128), F32)
        inner = jnp.zeros((TOK, 128), F32)
        for k in range(2):
            h = p * 2 + k
            own = jnp.where(lane < HEAD, 1.0 - k, float(k)).astype(BF16)
            vm, gm = vp * own, gp * own
            col = cumcol_ref[:, pl.ds(pl.multiple_of(h * 128, 128), 128)]
            row = cum_ref[pl.ds(h, 1), :]
            d00 = jnp.where(causal, jnp.exp(col[:128] - row[:, :128]), 0.0)
            d10 = jnp.exp(col[128:] - row[:, :128])
            d11 = jnp.where(causal, jnp.exp(col[128:] - row[:, 128:]), 0.0)
            grad = mm(gm, vp, NT)
            gsc_ref[:128, :128] += grad[:128, :128] * d00
            gsc_ref[128:, :128] += grad[128:, :128] * d10
            gsc_ref[128:, 128:] += grad[128:, 128:] * d11
            m00 = (sc_ref[:128, :128] * d00).astype(BF16)
            m10 = (sc_ref[128:, :128] * d10).astype(BF16)
            m11 = (sc_ref[128:, 128:] * d11).astype(BF16)
            mix = jnp.concatenate(
                [jnp.concatenate([m00, jnp.zeros_like(m00)], axis=1), jnp.concatenate([m10, m11], axis=1)], axis=0
            )
            intra = intra + mm(mix, vm, NN)
            inner = inner + mm(mix, gm, TN)
        intra_ref[:, at] = intra
        inner_ref[:, at] = inner
        w_ref[:, at] = gp.astype(F32) * intra - vp.astype(F32) * inner
        return carried

    def pairs(first, last):
        lax.fori_loop(first, last, pair, 0)

    def x_level(d, m):
        for j in x_peers:
            x_copy(d, m, j, j).wait_recv()
        state = jnp.zeros((CR, SL), F32)
        for i in range(NX) if d == 0 else range(NX - 1, -1, -1):
            pre_ref[d, m, i] = state
            state = xdr_ref[i, 0:1, :] * state + xr_ref[d, m, i]
        for i in range(NZ):
            zs_ref[d, m, i] = state[i * ZR : (i + 1) * ZR]
        for i in z_peers:
            z_copy(d, m, i, z).start()
        zr_ref[d, m, z] = zs_ref[d, m, z]

    def z_level(d, m):
        for i in z_peers:
            z_copy(d, m, i, i).wait_recv()
        state = jnp.zeros((ZR, SL), F32)
        for i in range(NZ) if d == 0 else range(NZ - 1, -1, -1):
            es_ref[d, m, i] = state
            state = zdr_ref[i, 0:1, :] * state + zr_ref[d, m, i]
        for i in z_peers:
            e_copy(d, m, i, z).start()
        er_ref[d, m, z] = es_ref[d, m, z]

    def back(d, m):
        for i in z_peers:
            e_copy(d, m, i, i).wait_recv()
        for n, j in enumerate(x_peers + [x]):
            through = cs_ref[d, j, 0:1, :]
            for i in range(NZ):
                rows = slice(i * ZR, (i + 1) * ZR)
                bs_ref[d, m, j, rows, :] = pre_ref[d, m, j, rows, :] + through * er_ref[d, m, i]
            if n < NX - 1:
                b_copy(d, m, j, x).start()
        br_ref[d, x, m * CR : (m + 1) * CR, :] = bs_ref[d, m, x]

    def arrived(d, j):
        for m in range(PIECES):
            b_copy(d, m, j, j).wait_recv()

    def ys_copy(d, j, i):
        return copy(ysum_ref.at[d, j], yr_ref.at[d, i], ys_sem.at[d, j], yr_sem.at[d, i], at_y(j))

    def ya_copy(d, j, i):
        return copy(ya_ref.at[d], yg_ref.at[d, i], as_sem.at[d, j], ar_sem.at[d, i], at_y(j))

    def y_scatter(d, part):
        for q in range(NY):
            ysum_ref[d, q] = part[q * (TOK // NY) : (q + 1) * (TOK // NY)]
        for q in y_peers:
            ys_copy(d, q, y).start()
        yr_ref[d, y] = ysum_ref[d, y]

    def y_gather(d):
        for q in y_peers:
            ys_copy(d, q, q).wait_recv()
        ya_ref[d] = (yr_ref[d, 0] + yr_ref[d, 1]) + (yr_ref[d, 2] + yr_ref[d, 3])
        for q in y_peers:
            ya_copy(d, q, y).start()
        yg_ref[d, y] = ya_ref[d]

    def y_finish(d, dst):
        for q in y_peers:
            ya_copy(d, q, q).wait_recv()
        for q in range(NY):
            dst[q * (TOK // NY) : (q + 1) * (TOK // NY), :] = yg_ref[d, q]

    pairs(0, 6)
    x_level(0, 0)
    pairs(6, 7)
    x_level(0, 1)
    z_level_decays = [zd_copy(i, i) for i in z_peers]
    for f in z_level_decays:
        f.wait_recv()
    z_level(0, 0)
    x_level(1, 0)
    z_level(0, 1)
    x_level(1, 1)
    back(0, 0)
    z_level(1, 0)
    pairs(7, 8)
    back(0, 1)
    z_level(1, 1)
    gsc_hi, gsc_lo = split2(gsc_ref[...])
    part_c = mm(gsc_hi, b, NN) + mm(gsc_lo, b, NN)
    part_b = mm(gsc_hi, c, TN) + mm(gsc_lo, c, TN)
    back(1, 0)
    back(1, 1)

    for n, j in enumerate([x] + x_peers[1:] + x_peers[:1]):
        if n:
            arrived(0, j)
        at = lanes(j)
        hi, lo = split2(br_ref[0, j])
        inter = mm(c, hi, NN) + mm(c, lo, NN)
        mamba = intra_ref[:, at] + grow_ref[:, at] * inter + skip_ref[:, at] * v_ref[:, at].astype(F32)
        gg_ref[:, at] = (gfac_ref[:, at] * mamba).astype(BF16)
        gi_hi, gi_lo = gihi_ref[:, at], gilo_ref[:, at]
        w_ref[:, at] += (gi_hi.astype(F32) + gi_lo.astype(F32)) * inter
        part_c = part_c + (mm(gi_hi, hi, NT) + mm(gi_lo, hi, NT) + mm(gi_hi, lo, NT))
    y_scatter(0, part_c)

    grad_cum = jnp.zeros((HEADS, TOK), F32)
    for n, j in enumerate([x] + x_peers[1:] + x_peers[:1]):
        if n:
            arrived(1, j)
        at = lanes(j)
        after = br_ref[1, j]
        hi, lo = split2(after)
        grad_scaled = mm(b, hi, NN) + mm(b, lo, NN)
        out_decay = decay_ref[:, at]
        gv_ref[:, at] = (inner_ref[:, at] + out_decay * grad_scaled + skip_ref[:, at] * gy_ref[:, at]).astype(BF16)
        from_scaled = grad_scaled * (out_decay * v_ref[:, at].astype(F32))
        last = jnp.sum(from_scaled, axis=0, keepdims=True)
        last = last + dw_ref[:, at] * jnp.sum(after * br_ref[0, j], axis=0, keepdims=True)
        w = w_ref[:, at] - from_scaled + jnp.where(iota((TOK, SL), 0) == TOK - 1, last, 0.0)
        start = iota((HEADS, SL), 0) * HEAD - j * SL
        lane = iota((HEADS, SL), 1)
        mark = jnp.where((lane >= start) & (lane < start + HEAD), 1.0, 0.0).astype(BF16)
        w_hi, w_mid, w_lo = split3(w)
        grad_cum = grad_cum + (mm(mark, w_hi, NT) + mm(mark, w_mid, NT) + mm(mark, w_lo, NT))
        scaled = scaled_ref[:, at]
        part_b = part_b + (mm(scaled, hi, NT) + mm(scaled, lo, NT))
    y_scatter(1, part_b)

    grad_log = lanes_cumsum(grad_cum, True)
    gs_ref[...] = -rate * grad_log
    rate_part = jnp.sum(-rate * steps * grad_log, axis=1, keepdims=True)
    skip_part = jnp.sum(jnp.where(marks, skipsum_ref[...], 0.0), axis=1, keepdims=True)
    own = r * NX + x
    same = iota((HEADS, 128), 0) == iota((HEADS, 128), 1)
    rate_row = jnp.sum(jnp.where(same, rate_part, 0.0), axis=0, keepdims=True)
    skip_row = jnp.sum(jnp.where(same, skip_part, 0.0), axis=0, keepdims=True)
    m1s_ref[...] = jnp.where(iota((8, 128), 0) == 0, rate_row, skip_row)
    m1_ref[own] = m1s_ref[...]
    near = [(r, p) for p in x_peers] + [(other, p) for p in x_peers + [x]]
    for rr, p in near:
        i = rr * NX + p
        copy(m1s_ref, m1_ref.at[own], m1s_sem.at[i], m1r_sem.at[own], (rr, z * NX + p, y)).start()
    y_gather(0)
    for rr, p in near:
        i = rr * NX + p
        copy(m1s_ref, m1_ref.at[i], m1s_sem.at[i], m1r_sem.at[i], (rr, z * NX + p, y)).wait_recv()
    m2s_ref[...] = ((m1_ref[0] + m1_ref[1]) + (m1_ref[2] + m1_ref[3])) + ((m1_ref[4] + m1_ref[5]) + (m1_ref[6] + m1_ref[7]))
    m2_ref[z] = m2s_ref[...]
    for i in z_peers:
        copy(m2s_ref, m2_ref.at[z], m2s_sem.at[i], m2r_sem.at[z], at_z(i)).start()
    y_gather(1)
    y_finish(0, gc_ref)
    y_finish(1, gb_ref)
    for i in z_peers:
        copy(m2s_ref, m2_ref.at[i], m2s_sem.at[i], m2r_sem.at[i], at_z(i)).wait_recv()
    small_ref[...] = ((m2_ref[0] + m2_ref[1]) + (m2_ref[2] + m2_ref[3])) + ((m2_ref[4] + m2_ref[5]) + (m2_ref[6] + m2_ref[7]))

    for d in range(2):
        for m in range(PIECES):
            for j in x_peers:
                x_copy(d, m, j, x).wait_send()
                b_copy(d, m, j, x).wait_send()
            for i in z_peers:
                z_copy(d, m, i, z).wait_send()
                e_copy(d, m, i, z).wait_send()
        for q in y_peers:
            ys_copy(d, q, y).wait_send()
            ya_copy(d, q, y).wait_send()
    for j in x_peers:
        xd_copy(j, x).wait_send()
    for i in z_peers:
        zd_copy(i, z).wait_send()
        copy(m2s_ref, m2_ref.at[z], m2s_sem.at[i], m2r_sem.at[z], at_z(i)).wait_send()
    for rr, p in near:
        i = rr * NX + p
        copy(m1s_ref, m1_ref.at[own], m1s_sem.at[i], m1r_sem.at[own], (rr, z * NX + p, y)).wait_send()


def leave(*refs):
    gv, gg, gb, gc, gs, small, gv_out, gg_out, gb_out, gc_out, gs_out, rate_out, skip_out, sem = refs
    moves = [
        pltpu.make_async_copy(src, dst, sem.at[i])
        for i, (src, dst) in enumerate(((gv, gv_out), (gg, gg_out), (gb, gb_out), (gc, gc_out), (gs, gs_out)))
    ]
    for move in moves:
        move.start()
    rate_out[...] = small[0:1, 0:HEADS]
    skip_out[...] = small[1:2, 0:HEADS]
    for move in moves:
        move.wait()


def block(values, gate_in, in_b, in_c, step_sizes, log_rates, skip_gain, grad_out):
    vmem = pl.BlockSpec(memory_space=pltpu.VMEM)
    anywhere = pl.BlockSpec(memory_space=pl.ANY)
    dma = pltpu.SemaphoreType.DMA
    wide, state = (TOK, WIDE), (TOK, STATE)
    scratch = [
        (wide, BF16), (wide, BF16), (state, BF16), (state, BF16), ((HEADS, TOK), F32), ((1, HEADS), F32), ((1, HEADS), F32),
        (wide, BF16),
        ((HEADS, TOK), F32), ((TOK, HEADS * 128), F32), (wide, F32), (wide, F32), ((1, WIDE), F32),
        (wide, BF16), (wide, F32), (wide, BF16), (wide, BF16), (wide, BF16),
        (wide, F32), ((TOK, TOK), F32), ((TOK, TOK), F32), (wide, F32), (wide, F32),
        (wide, F32), ((1, WIDE), F32), ((1, WIDE), F32),
        ((NX, 8, SL), F32), ((NX, 8, SL), F32), ((2, NX, 8, SL), F32), ((8, SL), F32), ((NZ, 8, SL), F32),
        ((2, PIECES, NX, CR, SL), F32), ((2, PIECES, NX, CR, SL), F32), ((2, PIECES, NX, CR, SL), F32),
        ((2, PIECES, NZ, ZR, SL), F32), ((2, PIECES, NZ, ZR, SL), F32), ((2, PIECES, NZ, ZR, SL), F32),
        ((2, PIECES, NZ, ZR, SL), F32),
        ((2, PIECES, NX, CR, SL), F32), ((2, NX, STATE, SL), F32),
        ((2, NY, TOK // NY, STATE), F32), ((2, NY, TOK // NY, STATE), F32), ((2, TOK // NY, STATE), F32),
        ((2, NY, TOK // NY, STATE), F32),
        ((8, 128), F32), ((NX * NR, 8, 128), F32), ((8, 128), F32), ((NZ, 8, 128), F32),
    ]
    xx, zz, yy = (2, PIECES, NX), (2, PIECES, NZ), (2, NY)
    sems = [(8,), (NX,), (NX,), (NZ,), (NZ,), xx, xx, zz, zz, zz, zz, xx, xx, yy, yy, yy, yy,
            (NX * NR,), (NX * NR,), (NZ,), (NZ,)]
    outs = [(wide, BF16), (wide, BF16), (state, F32), (state, F32), ((HEADS, TOK), F32)]
    held = pl.pallas_call(
        kernel,
        out_shape=[pltpu.VMEM(s, d) for s, d in outs + [((8, 128), F32)]],
        in_specs=[anywhere] * 8,
        out_specs=[vmem] * 6,
        scratch_shapes=[pltpu.VMEM(s, d) for s, d in scratch] + [dma(s) for s in sems],
        compiler_params=pltpu.CompilerParams(collective_id=0, has_side_effects=True),
    )(values[0], gate_in[0], in_b[0], in_c[0], step_sizes[0], log_rates[None], skip_gain[None], grad_out[0])
    gv, gg, gb, gc, gs, rates, skips = pl.pallas_call(
        leave,
        out_shape=[jax.ShapeDtypeStruct(s, d) for s, d in outs + [((1, HEADS), F32)] * 2],
        in_specs=[anywhere] * 5 + [vmem],
        out_specs=[anywhere] * 5 + [vmem] * 2,
        scratch_shapes=[dma((5,))],
        compiler_params=pltpu.CompilerParams(vmem_limit_bytes=1 << 20),
    )(*held)
    return gv[None], gg[None], gb[None], gc[None], gs[None], rates[0], skips[0]


def solution(mesh):
    wide = P("replica", "seq", "tensor")
    state = P("replica", "seq", None)
    step = P("replica", "tensor", "seq")
    head = P("tensor")
    return jax.shard_map(
        block,
        mesh=mesh,
        in_specs=(wide, wide, state, state, step, head, head, wide),
        out_specs=(wide, wide, state, state, step, head, head),
        check_vma=False,
    )
```

```python
import jax
import jax.numpy as jnp
from jax import lax
from jax.experimental import pallas as pl
from jax.experimental.pallas import tpu as pltpu
from jax.sharding import PartitionSpec as P

F32 = jnp.float32
BF16 = jnp.bfloat16
NX, NZ, NY, NR = 4, 8, 4, 2
HEADS, HEAD, STATE, TOK = 16, 64, 128, 256
WIDE = HEADS * HEAD
SL = WIDE // NX
PIECES = 4
CR = STATE // PIECES
QT = TOK // NY
NT = (((1,), (1,)), ((), ()))
TN = (((0,), (0,)), ((), ()))
NN = (((1,), (0,)), ((), ()))


def mm(a, b, dims):
    return lax.dot_general(a, b, dims, preferred_element_type=F32)


def split2(x):
    hi = x.astype(BF16)
    return hi, (x - hi.astype(F32)).astype(BF16)


def split3(x):
    hi = x.astype(BF16)
    rest = x - hi.astype(F32)
    mid = rest.astype(BF16)
    return hi, mid, (rest - mid.astype(F32)).astype(BF16)


def iota(shape, dim):
    return lax.broadcasted_iota(jnp.int32, shape, dim)


def column(row):
    n = row.shape[1]
    same = iota((n, n), 0) == iota((n, n), 1)
    return jnp.sum(jnp.where(same, jnp.broadcast_to(row, (n, n)), 0.0), axis=1, keepdims=True)


def lanes_cumsum(x, reverse):
    n = x.shape[1]
    lane = iota(x.shape, 1)
    by = 1
    while by < n:
        if reverse:
            x = x + jnp.where(lane < n - by, pltpu.roll(x, n - by, 1), 0.0)
        else:
            x = x + jnp.where(lane >= by, pltpu.roll(x, by, 1), 0.0)
        by *= 2
    return x


def head_rows(rows, width):
    shape = (rows, rows * width)
    start = iota(shape, 0) * width
    lane = iota(shape, 1)
    return (lane >= start) & (lane < start + width)


def kernel(
    v_hbm, g_hbm, b_hbm, c_hbm, st_hbm, lr_hbm, sg_hbm, go_hbm,
    gv_ref, gg_ref, gb_ref, gc_ref, gs_ref, rate_ref, skp_ref,
    v_ref, g_ref, b_ref, c_ref, st_ref, lr_ref, sg_ref, go_ref,
    cum_ref, cumcol_ref, grow_ref, decay_ref, skip_ref, scaled_ref, gy_ref, gyb_ref, gihi_ref, gilo_ref,
    gfac_ref, sc_ref, gsc_ref, intra_ref, inner_ref, w_ref, dw_ref, skipsum_ref, cumw_ref, tot_ref, rsum_ref, mom_ref, sta_ref,
    xd_ref, xdr_ref, cs_ref, zd_ref, zdr_ref,
    xs_ref, xr_ref, pre_ref, zs_ref, zr_ref, es_ref, er_ref, bs_ref, br_ref,
    ysum_ref, yr_ref, ya_ref, yg_ref, hs_ref, hr_ref, m1s_ref, m1_ref, m2s_ref, m2_ref,
    in_sem, out_sem, one_sem, xr_sem, zr_sem, er_sem, br_sem, hr_sem,
):
    r = lax.axis_index("replica")
    seq = lax.axis_index("seq")
    y = lax.axis_index("tensor")
    z, x = seq // NX, seq % NX

    fetch = [
        pltpu.make_async_copy(src, dst, in_sem.at[i])
        for i, (src, dst) in enumerate((
            (lr_hbm, lr_ref), (st_hbm, st_ref), (b_hbm, b_ref), (v_hbm, v_ref),
            (c_hbm, c_ref), (g_hbm, g_ref), (go_hbm, go_ref), (sg_hbm, sg_ref),
        ))
    ]
    for f in fetch:
        f.start()

    barrier = pltpu.get_barrier_semaphore()

    def at_x(to):
        return (r, z * NX + to, y)

    def at_z(to):
        return (r, to * NX + x, y)

    def at_y(to):
        return (r, seq, to)

    x_peers = [(x + o) % NX for o in (2, 1, 3)]
    z_peers = [(z + o) % NZ for o in (4, 3, 5, 2, 6, 1, 7)]
    y_peers = [(y + o) % NY for o in (2, 1, 3)]
    other = (r + 1) % NR
    met = [at_z(p) for p in z_peers] + [at_x(p) for p in x_peers] + [at_y(p) for p in y_peers]
    met += [(other, z * NX + p, y) for p in x_peers + [x]]
    for device in met:
        pl.semaphore_signal(barrier, inc=1, device_id=device, device_id_type=pl.DeviceIdType.MESH)

    def copy(src, dst, s, d, device):
        return pltpu.make_async_remote_copy(
            src_ref=src, dst_ref=dst, send_sem=s, recv_sem=d,
            device_id=device, device_id_type=pl.DeviceIdType.MESH,
        )

    later = iota((TOK, TOK), 0) > iota((TOK, TOK), 1)
    later_b = jnp.where(later, 1.0, 0.0).astype(BF16)

    def thirds(p):
        return (p[:HEADS] + p[HEADS : 2 * HEADS]) + p[2 * HEADS :]

    def spread_marks(j):
        start = (iota((3 * HEADS, SL), 0) % HEADS) * HEAD - j * SL
        lane = iota((3 * HEADS, SL), 1)
        return jnp.where((lane >= start) & (lane < start + HEAD), 1.0, 0.0).astype(BF16)

    for f in fetch[:2]:
        f.wait()
    rate = jnp.exp(column(lr_ref[...]))
    steps = st_ref[...]
    log = -rate * steps
    log3 = jnp.concatenate(split3(log), axis=0)
    suffix = thirds(mm(log3, later_b, NN))
    decay3 = jnp.concatenate(split3(jnp.exp(suffix)), axis=0)
    total = suffix[:, 0:1] + log[:, 0:1]
    marks = head_rows(HEADS, HEAD)
    marks_f = jnp.where(marks, 1.0, 0.0)
    dw_ref[...] = jnp.sum(marks_f * jnp.exp(total), axis=0, keepdims=True)
    for j in range(NX):
        xd_ref[j] = jnp.broadcast_to(dw_ref[:, j * SL : (j + 1) * SL], (8, SL))
    for f in fetch[2:4]:
        f.wait()
    b = b_ref[...]

    def lanes(j):
        return pl.ds(pl.multiple_of(j * SL, SL), SL)

    def keep(d, j, state):
        for m in range(PIECES):
            xs_ref[d, m, j] = state[m * CR : (m + 1) * CR]

    def x_copy(d, m, j):
        return copy(xs_ref.at[d, m, j], xr_ref.at[d, m, x], out_sem.at[0], xr_sem.at[d, m], at_x(j))

    def b_copy(d, m, j):
        return copy(bs_ref.at[d, m, j], br_ref.at[d, x, pl.ds(m * CR, CR)], out_sem.at[1], br_sem.at[d, m], at_x(j))

    def z_copy(d, m, j):
        return copy(zs_ref.at[d, m, j], zr_ref.at[d, m, z], out_sem.at[2], zr_sem.at[d, m], at_z(j))

    def e_copy(d, m, j):
        return copy(es_ref.at[d, m, j], er_ref.at[d, m, z], out_sem.at[3], er_sem.at[d, m], at_z(j))

    def xd_copy(j):
        return copy(xd_ref.at[j], xdr_ref.at[x], out_sem.at[4], one_sem.at[0], at_x(j))

    def zd_copy(j):
        return copy(zd_ref, zdr_ref.at[z], out_sem.at[5], one_sem.at[1], at_z(j))

    def ys_copy(j):
        return copy(ysum_ref.at[j], yr_ref.at[y], out_sem.at[6], one_sem.at[2], at_y(j))

    def ya_copy(j):
        return copy(ya_ref, yg_ref.at[y], out_sem.at[7], one_sem.at[3], at_y(j))

    def h_copy(m, j):
        return copy(hs_ref.at[m], hr_ref.at[m, y], out_sem.at[8], hr_sem.at[m], at_y(j))

    def m1_copy(rr, p):
        return copy(m1s_ref, m1_ref.at[own], out_sem.at[9], one_sem.at[4], (rr, z * NX + p, y))

    def m2_copy(j):
        return copy(m2s_ref, m2_ref.at[z], out_sem.at[10], one_sem.at[5], at_z(j))

    def got(ref, sem):
        copy(ref, ref, out_sem.at[0], sem, at_x(x_peers[0])).wait_recv()

    def sent(ref, kind):
        copy(ref, ref, out_sem.at[kind], one_sem.at[0], at_x(x_peers[0])).wait_send()

    few, many = pl.ds(0, NX - 1), pl.ds(0, NZ - 1)
    own = r * NX + x

    for n, j in enumerate(x_peers + [x]):
        at = lanes(j)
        decay = mm(decay3, spread_marks(j), TN)
        decay_ref[:, at] = decay
        scaled = (decay * v_ref[:, at].astype(F32)).astype(BF16)
        scaled_ref[:, at] = scaled
        keep(0, j, mm(b, scaled, TN))
        if n == 0:
            pl.semaphore_wait(barrier, len(met))
            for i in x_peers:
                xd_copy(i).start()
        if n < NX - 1:
            x_copy(0, 0, j).start()
    for m in range(1, PIECES):
        for j in x_peers:
            x_copy(0, m, j).start()
    xdr_ref[x] = xd_ref[x]

    cum = thirds(mm(log3, 1.0 - later_b, NN))
    cum_ref[...] = cum
    marks_b = marks_f.astype(BF16)
    marks3 = jnp.concatenate([marks_b, marks_b, marks_b], axis=0)
    grow_ref[...] = mm(jnp.concatenate(split3(jnp.exp(cum)), axis=0), marks3, TN)
    for f in fetch[4:]:
        f.wait()
    c = c_ref[...]
    for n, j in enumerate(x_peers + [x]):
        at = lanes(j)
        gate = g_ref[:, at].astype(F32)
        sig = 1.0 / (1.0 + jnp.exp(-gate))
        out = go_ref[:, at].astype(F32)
        gy = out * (gate * sig)
        gy_ref[:, at] = gy
        gyb_ref[:, at] = gy.astype(BF16)
        gfac_ref[:, at] = out * sig * (1.0 + gate * (1.0 - sig))
        hi, lo = split2(grow_ref[:, at] * gy)
        gihi_ref[:, at] = hi
        gilo_ref[:, at] = lo
        keep(1, j, mm(c, hi, TN) + mm(c, lo, TN))
        if n < NX - 1:
            x_copy(1, 0, j).start()
        skipsum_ref[:, at] = jnp.sum(gy * v_ref[:, at].astype(F32), axis=0, keepdims=True)
    for m in range(1, PIECES):
        for j in x_peers:
            x_copy(1, m, j).start()
    for d in range(2):
        for m in range(PIECES):
            xr_ref[d, m, x] = xs_ref[d, m, x]

    got(xdr_ref.at[few], one_sem.at[0])
    for d in range(2):
        through = jnp.ones((8, SL), F32)
        for i in range(NX) if d == 0 else range(NX - 1, -1, -1):
            cs_ref[d, i] = through
            through = through * xdr_ref[i]
        if d == 0:
            zd_ref[...] = through
    zdr_ref[z] = zd_ref[...]
    for i in z_peers:
        zd_copy(i).start()

    sc_ref[...] = mm(c, b, NT)
    gsc_ref[...] = jnp.zeros_like(gsc_ref)
    cum3 = jnp.concatenate(split3(cum), axis=0)
    wide = jnp.where(head_rows(HEADS, 128), 1.0, 0.0).astype(BF16)
    cumcol_ref[...] = mm(cum3, jnp.concatenate([wide] * 3, axis=0), TN)
    cumw_ref[...] = mm(cum3, marks3, TN)
    tot_ref[...] = jnp.sum(marks_f * total, axis=0, keepdims=True)
    skip_ref[...] = jnp.sum(marks_f * column(sg_ref[...]), axis=0, keepdims=True)

    def pair(p, carried):
        at = pl.ds(pl.multiple_of(p * 128, 128), 128)
        vp, gp = v_ref[:, at], gyb_ref[:, at]
        lane = iota((TOK, 128), 1)
        causal = iota((128, 128), 0) >= iota((128, 128), 1)
        intra = jnp.zeros((TOK, 128), F32)
        inner = jnp.zeros((TOK, 128), F32)
        for k in range(2):
            h = p * 2 + k
            own = jnp.where(lane < HEAD, 1.0 - k, float(k)).astype(BF16)
            vm, gm = vp * own, gp * own
            col = cumcol_ref[:, pl.ds(pl.multiple_of(h * 128, 128), 128)]
            row = cum_ref[pl.ds(h, 1), :]
            d00 = jnp.where(causal, jnp.exp(col[:128] - row[:, :128]), 0.0)
            d10 = jnp.exp(col[128:] - row[:, :128])
            d11 = jnp.where(causal, jnp.exp(col[128:] - row[:, 128:]), 0.0)
            grad = mm(gm, vp, NT)
            gsc_ref[:128, :128] += grad[:128, :128] * d00
            gsc_ref[128:, :128] += grad[128:, :128] * d10
            gsc_ref[128:, 128:] += grad[128:, 128:] * d11
            m00 = (sc_ref[:128, :128] * d00).astype(BF16)
            m10 = (sc_ref[128:, :128] * d10).astype(BF16)
            m11 = (sc_ref[128:, 128:] * d11).astype(BF16)
            mix = jnp.concatenate(
                [jnp.concatenate([m00, jnp.zeros_like(m00)], axis=1), jnp.concatenate([m10, m11], axis=1)], axis=0
            )
            intra = intra + mm(mix, vm, NN)
            inner = inner + mm(mix, gm, TN)
        intra_ref[:, at] = intra
        inner_ref[:, at] = inner
        w_ref[:, at] = gp.astype(F32) * intra - vp.astype(F32) * inner
        return carried

    def pairs(first, last):
        lax.fori_loop(first, last, pair, 0)

    def tile(i):
        return slice(i % 4 * 8, i % 4 * 8 + 8), slice(i // 4 * 128, i // 4 * 128 + 128)

    mine = pl.ds(pl.multiple_of(z // 4 * 128, 128), 128)

    def x_level(d, m):
        got(xr_ref.at[d, m, few], xr_sem.at[d, m])
        state = jnp.zeros((CR, SL), F32)
        for i in range(NX) if d == 0 else range(NX - 1, -1, -1):
            pre_ref[d, m, i] = state
            state = xdr_ref[i, 0:1, :] * state + xr_ref[d, m, i]
        for i in range(NZ):
            zs_ref[d, m, i] = state[tile(i)]
        for i in z_peers:
            z_copy(d, m, i).start()
        zr_ref[d, m, z] = zs_ref[d, m, z]

    def z_level(d, m):
        got(zr_ref.at[d, m, many], zr_sem.at[d, m])
        state = jnp.zeros((8, 128), F32)
        for i in range(NZ) if d == 0 else range(NZ - 1, -1, -1):
            es_ref[d, m, i] = state
            state = zdr_ref[i, :, mine] * state + zr_ref[d, m, i]
        for i in z_peers:
            e_copy(d, m, i).start()
        er_ref[d, m, z] = es_ref[d, m, z]

    def back(d, m):
        got(er_ref.at[d, m, many], er_sem.at[d, m])
        for n, j in enumerate(x_peers + [x]):
            through = cs_ref[d, j, 0:1, :]
            for i in range(NZ):
                rows, cols = tile(i)
                bs_ref[d, m, j, rows, cols] = pre_ref[d, m, j, rows, cols] + through[:, cols] * er_ref[d, m, i]
            if n < NX - 1:
                b_copy(d, m, j).start()
        br_ref[d, x, m * CR : (m + 1) * CR, :] = bs_ref[d, m, x]

    def arrived(d, m):
        got(br_ref.at[d, 0, pl.ds(0, (NX - 1) * CR)], br_sem.at[d, m])

    pairs(0, 4)
    for m in range(PIECES):
        x_level(0, m)
        pairs(4 + m, 5 + m)
    got(zdr_ref.at[many], one_sem.at[1])
    z_level(0, 0)
    x_level(1, 0)
    z_level(0, 1)
    x_level(1, 1)
    z_level(0, 2)
    x_level(1, 2)
    z_level(0, 3)
    back(0, 0)
    x_level(1, 3)
    z_level(1, 0)
    back(0, 1)
    z_level(1, 1)
    back(0, 2)
    z_level(1, 2)
    back(0, 3)
    z_level(1, 3)
    gsc_hi, gsc_lo = split2(gsc_ref[...])
    part_c = mm(gsc_hi, b, NN) + mm(gsc_lo, b, NN)
    part_b = mm(c, gsc_hi, TN) + mm(c, gsc_lo, TN)

    def moments(j):
        at = slice(j * SL, (j + 1) * SL)
        exact = decay_ref[:, at] * v_ref[:, at].astype(F32)
        for dst, what in ((sta_ref, exact), (mom_ref, exact * cumw_ref[:, at])):
            p0, p1, p2 = split3(what)
            dst[:, at] = mm(b, p0, TN) + mm(b, p1, TN) + mm(b, p2, TN)

    back(1, 0)
    moments(0)
    moments(1)
    back(1, 1)
    moments(2)
    moments(3)
    back(1, 2)
    back(1, 3)

    for m in range(PIECES):
        arrived(0, m)
    for j in range(NX):
        at = slice(j * SL, (j + 1) * SL)
        enter = br_ref[0, j]
        hi, lo = split2(enter)
        inter = mm(c, hi, NN) + mm(c, lo, NN)
        mamba = intra_ref[:, at] + grow_ref[:, at] * inter + skip_ref[:, at] * v_ref[:, at].astype(F32)
        gg_ref[:, at] = (gfac_ref[:, at] * mamba).astype(BF16)
        gi_hi, gi_lo = gihi_ref[:, at], gilo_ref[:, at]
        w = w_ref[:, at] + (gi_hi.astype(F32) + gi_lo.astype(F32)) * inter
        w_ref[:, at] = w
        rsum_ref[:, at] = jnp.sum(w * cumw_ref[:, at], axis=0, keepdims=True)
        mom_ref[:, at] = tot_ref[:, at] * (sta_ref[:, at] + dw_ref[:, at] * enter) - mom_ref[:, at]
        part_c = part_c + (mm(gi_hi, hi, NT) + mm(gi_lo, hi, NT) + mm(gi_hi, lo, NT))
    for q in range(NY):
        ysum_ref[q] = part_c[q * QT : (q + 1) * QT]
    for q in y_peers:
        ys_copy(q).start()
    yr_ref[y] = ysum_ref[y]

    def piece_b(m):
        rows = slice(m * CR, (m + 1) * CR)
        both = jnp.zeros((2 * CR, TOK), F32)
        for j in range(NX):
            pair_b = jnp.concatenate(split2(br_ref[1, j, rows, :]), axis=0)
            both = both + mm(pair_b, scaled_ref[:, j * SL : (j + 1) * SL], NT)
        hs_ref[m] = part_b[rows] + (both[:CR] + both[CR:])
        for q in y_peers:
            h_copy(m, q).start()
        hr_ref[m, y] = hs_ref[m]

    for m in range(PIECES - 1):
        arrived(1, m)
        piece_b(m)
    arrived(1, PIECES - 1)
    for j in range(NX):
        at = slice(j * SL, (j + 1) * SL)
        rsum_ref[:, at] += jnp.sum(br_ref[1, j] * mom_ref[:, at], axis=0, keepdims=True)

    rate_part = jnp.sum(jnp.where(marks, rsum_ref[...], 0.0), axis=1, keepdims=True)
    skip_part = jnp.sum(jnp.where(marks, skipsum_ref[...], 0.0), axis=1, keepdims=True)
    same = iota((HEADS, 128), 0) == iota((HEADS, 128), 1)
    rate_row = jnp.sum(jnp.where(same, rate_part, 0.0), axis=0, keepdims=True)
    skip_row = jnp.sum(jnp.where(same, skip_part, 0.0), axis=0, keepdims=True)
    m1s_ref[...] = jnp.where(iota((8, 128), 0) == 0, rate_row, skip_row)
    near = [(r, p) for p in x_peers] + [(other, p) for p in x_peers + [x]]
    for rr, p in near:
        m1_copy(rr, p).start()
    m1_ref[own] = m1s_ref[...]
    piece_b(PIECES - 1)

    for j in range(NX):
        at = slice(j * SL, (j + 1) * SL)
        after = br_ref[1, j]
        hi, lo = split2(after)
        grad_scaled = mm(b, hi, NN) + mm(b, lo, NN)
        out_decay = decay_ref[:, at]
        gv_ref[:, at] = (inner_ref[:, at] + out_decay * grad_scaled + skip_ref[:, at] * gy_ref[:, at]).astype(BF16)
        from_scaled = grad_scaled * (out_decay * v_ref[:, at].astype(F32))
        last = jnp.sum(from_scaled, axis=0, keepdims=True)
        last = last + dw_ref[:, at] * jnp.sum(after * br_ref[0, j], axis=0, keepdims=True)
        w_ref[:, at] = w_ref[:, at] - from_scaled
        w_ref[TOK - 1 : TOK, at] += last
    got(yr_ref.at[few], one_sem.at[2])
    ya_ref[...] = (yr_ref[0] + yr_ref[1]) + (yr_ref[2] + yr_ref[3])
    for q in y_peers:
        ya_copy(q).start()
    yg_ref[y] = ya_ref[...]
    got(m1_ref.at[pl.ds(0, NX * NR - 1)], one_sem.at[4])
    m2s_ref[...] = ((m1_ref[0] + m1_ref[1]) + (m1_ref[2] + m1_ref[3])) + ((m1_ref[4] + m1_ref[5]) + (m1_ref[6] + m1_ref[7]))
    for i in z_peers:
        m2_copy(i).start()
    m2_ref[z] = m2s_ref[...]
    grad_cum = jnp.zeros((HEADS, TOK), F32)
    for j in range(NX):
        at = slice(j * SL, (j + 1) * SL)
        mark = marks_b[:, at]
        w_hi, w_mid, w_lo = split3(w_ref[:, at])
        grad_cum = grad_cum + (mm(mark, w_hi, NT) + mm(mark, w_mid, NT) + mm(mark, w_lo, NT))
    gs_ref[...] = -rate * lanes_cumsum(grad_cum, True)
    for m in range(PIECES):
        got(hr_ref.at[m, few], hr_sem.at[m])
    gb_ref[...] = jnp.concatenate(
        [(hr_ref[m, 0] + hr_ref[m, 1]) + (hr_ref[m, 2] + hr_ref[m, 3]) for m in range(PIECES)], axis=0
    ).T
    got(yg_ref.at[few], one_sem.at[3])
    for q in range(NY):
        gc_ref[q * QT : (q + 1) * QT, :] = yg_ref[q]
    got(m2_ref.at[many], one_sem.at[5])
    sums = ((m2_ref[0] + m2_ref[1]) + (m2_ref[2] + m2_ref[3])) + ((m2_ref[4] + m2_ref[5]) + (m2_ref[6] + m2_ref[7]))
    rate_ref[...] = sums[0:1, 0:HEADS]
    skp_ref[...] = sums[1:2, 0:HEADS]

    sent(xs_ref.at[:, :, few], 0)
    sent(bs_ref.at[:, :, few], 1)
    sent(zs_ref.at[:, :, many], 2)
    sent(es_ref.at[:, :, many], 3)
    sent(xd_ref.at[few], 4)
    sent(zdr_ref.at[many], 5)
    sent(ysum_ref.at[few], 6)
    sent(yg_ref.at[few], 7)
    sent(hr_ref.at[:, few], 8)
    sent(m1_ref.at[pl.ds(0, NX * NR - 1)], 9)
    sent(m2_ref.at[many], 10)


def leave(*refs):
    count = len(refs) // 2
    moves = [pltpu.make_async_copy(refs[i], refs[count + i], refs[-1].at[i]) for i in range(count)]
    for move in moves:
        move.start()
    for move in moves:
        move.wait()


def block(values, gate_in, in_b, in_c, step_sizes, log_rates, skip_gain, grad_out):
    vmem = pl.BlockSpec(memory_space=pltpu.VMEM)
    anywhere = pl.BlockSpec(memory_space=pl.ANY)
    dma = pltpu.SemaphoreType.DMA
    wide, state = (TOK, WIDE), (TOK, STATE)
    scratch = [
        (wide, BF16), (wide, BF16), (state, BF16), (state, BF16), ((HEADS, TOK), F32), ((1, HEADS), F32), ((1, HEADS), F32),
        (wide, BF16),
        ((HEADS, TOK), F32), ((TOK, HEADS * 128), F32), (wide, F32), (wide, F32), ((1, WIDE), F32),
        (wide, BF16), (wide, F32), (wide, BF16), (wide, BF16), (wide, BF16),
        (wide, F32), ((TOK, TOK), F32), ((TOK, TOK), F32), (wide, F32), (wide, F32),
        (wide, F32), ((1, WIDE), F32), ((1, WIDE), F32), (wide, F32), ((1, WIDE), F32), ((1, WIDE), F32), ((STATE, WIDE), F32),
        ((STATE, WIDE), F32),
        ((NX, 8, SL), F32), ((NX, 8, SL), F32), ((2, NX, 8, SL), F32), ((8, SL), F32), ((NZ, 8, SL), F32),
        ((2, PIECES, NX, CR, SL), F32), ((2, PIECES, NX, CR, SL), F32), ((2, PIECES, NX, CR, SL), F32),
        ((2, PIECES, NZ, 8, 128), F32), ((2, PIECES, NZ, 8, 128), F32), ((2, PIECES, NZ, 8, 128), F32),
        ((2, PIECES, NZ, 8, 128), F32),
        ((2, PIECES, NX, CR, SL), F32), ((2, NX, STATE, SL), F32),
        ((NY, QT, STATE), F32), ((NY, QT, STATE), F32), ((QT, STATE), F32), ((NY, QT, STATE), F32),
        ((PIECES, CR, TOK), F32), ((PIECES, NY, CR, TOK), F32),
        ((8, 128), F32), ((NX * NR, 8, 128), F32), ((8, 128), F32), ((NZ, 8, 128), F32),
    ]
    sems = [(8,), (11,), (6,)] + [(2, PIECES)] * 4 + [(PIECES,)]
    outs = [(wide, BF16), (wide, BF16), (state, F32), (state, F32), ((HEADS, TOK), F32)] + [((1, HEADS), F32)] * 2
    held = pl.pallas_call(
        kernel,
        out_shape=[pltpu.VMEM(s, d) for s, d in outs],
        in_specs=[anywhere] * 8,
        out_specs=[vmem] * len(outs),
        scratch_shapes=[pltpu.VMEM(s, d) for s, d in scratch] + [dma(s) for s in sems],
        compiler_params=pltpu.CompilerParams(collective_id=0, has_side_effects=True),
    )(values[0], gate_in[0], in_b[0], in_c[0], step_sizes[0], log_rates[None], skip_gain[None], grad_out[0])
    gv, gg, gb, gc, gs, rates, skips = pl.pallas_call(
        leave,
        out_shape=[jax.ShapeDtypeStruct(s, d) for s, d in outs],
        in_specs=[anywhere] * len(outs),
        out_specs=[anywhere] * len(outs),
        scratch_shapes=[dma((len(outs),))],
        compiler_params=pltpu.CompilerParams(vmem_limit_bytes=1 << 20),
    )(*held)
    return gv[None], gg[None], gb[None], gc[None], gs[None], rates[0], skips[0]


def solution(mesh):
    wide = P("replica", "seq", "tensor")
    state = P("replica", "seq", None)
    step = P("replica", "tensor", "seq")
    head = P("tensor")
    return jax.shard_map(
        block,
        mesh=mesh,
        in_specs=(wide, wide, state, state, step, head, head, wide),
        out_specs=(wide, wide, state, state, step, head, head),
        check_vma=False,
    )
```

```python
import jax
import jax.numpy as jnp
from jax import lax
from jax.experimental import pallas as pl
from jax.experimental.pallas import tpu as pltpu
from jax.sharding import PartitionSpec as P

F32 = jnp.float32
BF16 = jnp.bfloat16
NX, NZ, NY, NR = 4, 8, 4, 2
HEADS, HEAD, STATE, TOK = 16, 64, 128, 256
WIDE = HEADS * HEAD
SL = WIDE // NX
PIECES = 4
CR = STATE // PIECES
QT = TOK // NY
NT = (((1,), (1,)), ((), ()))
TN = (((0,), (0,)), ((), ()))
NN = (((1,), (0,)), ((), ()))


def mm(a, b, dims):
    return lax.dot_general(a, b, dims, preferred_element_type=F32)


def split2(x):
    hi = x.astype(BF16)
    return hi, (x - hi.astype(F32)).astype(BF16)


def split3(x):
    hi = x.astype(BF16)
    rest = x - hi.astype(F32)
    mid = rest.astype(BF16)
    return hi, mid, (rest - mid.astype(F32)).astype(BF16)


def iota(shape, dim):
    return lax.broadcasted_iota(jnp.int32, shape, dim)


def column(row):
    n = row.shape[1]
    same = iota((n, n), 0) == iota((n, n), 1)
    return jnp.sum(jnp.where(same, jnp.broadcast_to(row, (n, n)), 0.0), axis=1, keepdims=True)


def lanes_cumsum(x, reverse):
    n = x.shape[1]
    lane = iota(x.shape, 1)
    by = 1
    while by < n:
        if reverse:
            x = x + jnp.where(lane < n - by, pltpu.roll(x, n - by, 1), 0.0)
        else:
            x = x + jnp.where(lane >= by, pltpu.roll(x, by, 1), 0.0)
        by *= 2
    return x


def head_rows(rows, width):
    shape = (rows, rows * width)
    start = iota(shape, 0) * width
    lane = iota(shape, 1)
    return (lane >= start) & (lane < start + width)


def kernel(
    v_hbm, g_hbm, b_hbm, c_hbm, st_hbm, lr_hbm, sg_hbm, go_hbm,
    gv_ref, gg_ref, gb_ref, gc_ref, gs_ref, rate_ref, skp_ref,
    v_ref, g_ref, b_ref, c_ref, st_ref, lr_ref, sg_ref, go_ref,
    cum_ref, cumcol_ref, grow_ref, decay_ref, skip_ref, scaled_ref, gy_ref, gyb_ref, gihi_ref, gilo_ref,
    gfac_ref, sc_ref, gsc_ref, intra_ref, inner_ref, w_ref, dw_ref, skipsum_ref, cumw_ref, tot_ref, rsum_ref, mom_ref, sta_ref,
    xd_ref, xdr_ref, cs_ref, zd_ref, zdr_ref,
    xs_ref, xr_ref, pre_ref, zs_ref, zr_ref, es_ref, er_ref, bs_ref, br_ref,
    ysum_ref, yr_ref, ya_ref, yg_ref, hs_ref, hr_ref, m1s_ref, m1_ref, m2s_ref, m2_ref,
    in_sem, out_sem, one_sem, xr_sem, zr_sem, er_sem, br_sem, hr_sem,
):
    r = lax.axis_index("replica")
    seq = lax.axis_index("seq")
    y = lax.axis_index("tensor")
    z, x = seq // NX, seq % NX

    fetch = [
        pltpu.make_async_copy(src, dst, in_sem.at[i])
        for i, (src, dst) in enumerate((
            (lr_hbm, lr_ref), (st_hbm, st_ref), (b_hbm, b_ref), (v_hbm, v_ref),
            (c_hbm, c_ref), (g_hbm, g_ref), (go_hbm, go_ref), (sg_hbm, sg_ref),
        ))
    ]
    for f in fetch:
        f.start()

    barrier = pltpu.get_barrier_semaphore()

    def at_x(to):
        return (r, z * NX + to, y)

    def at_z(to):
        return (r, to * NX + x, y)

    def at_y(to):
        return (r, seq, to)

    x_peers = [(x + o) % NX for o in (2, 1, 3)]
    z_peers = [(z + o) % NZ for o in (4, 3, 5, 2, 6, 1, 7)]
    y_peers = [(y + o) % NY for o in (2, 1, 3)]
    other = (r + 1) % NR
    met = [at_z(p) for p in z_peers] + [at_x(p) for p in x_peers] + [at_y(p) for p in y_peers]
    met += [(other, z * NX + p, y) for p in x_peers + [x]]
    for device in met:
        pl.semaphore_signal(barrier, inc=1, device_id=device, device_id_type=pl.DeviceIdType.MESH)

    def copy(src, dst, s, d, device):
        return pltpu.make_async_remote_copy(
            src_ref=src, dst_ref=dst, send_sem=s, recv_sem=d,
            device_id=device, device_id_type=pl.DeviceIdType.MESH,
        )

    later = iota((TOK, TOK), 0) > iota((TOK, TOK), 1)
    later_b = jnp.where(later, 1.0, 0.0).astype(BF16)

    def thirds(p):
        return (p[:HEADS] + p[HEADS : 2 * HEADS]) + p[2 * HEADS :]

    def spread_marks(j):
        start = (iota((3 * HEADS, SL), 0) % HEADS) * HEAD - j * SL
        lane = iota((3 * HEADS, SL), 1)
        return jnp.where((lane >= start) & (lane < start + HEAD), 1.0, 0.0).astype(BF16)

    for f in fetch[:2]:
        f.wait()
    rate = jnp.exp(column(lr_ref[...]))
    steps = st_ref[...]
    log = -rate * steps
    log3 = jnp.concatenate(split3(log), axis=0)
    suffix = thirds(mm(log3, later_b, NN))
    decay3 = jnp.concatenate(split3(jnp.exp(suffix)), axis=0)
    total = suffix[:, 0:1] + log[:, 0:1]
    marks = head_rows(HEADS, HEAD)
    marks_f = jnp.where(marks, 1.0, 0.0)
    dw_ref[...] = jnp.sum(marks_f * jnp.exp(total), axis=0, keepdims=True)
    for j in range(NX):
        xd_ref[j] = dw_ref[:, j * SL : (j + 1) * SL]
    for f in fetch[2:4]:
        f.wait()
    b = b_ref[...]

    def lanes(j):
        return pl.ds(pl.multiple_of(j * SL, SL), SL)

    def keep(d, j, state):
        for m in range(PIECES):
            xs_ref[d, m, j] = state[m * CR : (m + 1) * CR]

    def x_copy(d, m, j):
        return copy(xs_ref.at[d, m, j], xr_ref.at[d, m, x], out_sem.at[0], xr_sem.at[d, m], at_x(j))

    def b_copy(d, m, j):
        return copy(bs_ref.at[d, m, j], br_ref.at[d, x, pl.ds(m * CR, CR)], out_sem.at[1], br_sem.at[d, m], at_x(j))

    def z_copy(d, m, j):
        return copy(zs_ref.at[d, m, j], zr_ref.at[d, m, z], out_sem.at[2], zr_sem.at[d, m], at_z(j))

    def e_copy(d, m, j):
        return copy(es_ref.at[d, m, j], er_ref.at[d, m, z], out_sem.at[3], er_sem.at[d, m], at_z(j))

    def xd_copy(j):
        return copy(xd_ref.at[j], xdr_ref.at[x], out_sem.at[4], one_sem.at[0], at_x(j))

    def zd_copy(j):
        return copy(zd_ref, zdr_ref.at[z], out_sem.at[5], one_sem.at[1], at_z(j))

    def ys_copy(j):
        return copy(ysum_ref.at[j], yr_ref.at[y], out_sem.at[6], one_sem.at[2], at_y(j))

    def ya_copy(j):
        return copy(ya_ref, yg_ref.at[y], out_sem.at[7], one_sem.at[3], at_y(j))

    def h_copy(m, j):
        return copy(hs_ref.at[m], hr_ref.at[m, y], out_sem.at[8], hr_sem.at[m], at_y(j))

    def m1_copy(rr, p):
        return copy(m1s_ref, m1_ref.at[own], out_sem.at[9], one_sem.at[4], (rr, z * NX + p, y))

    def m2_copy(j):
        return copy(m2s_ref, m2_ref.at[z], out_sem.at[10], one_sem.at[5], at_z(j))

    def got(ref, sem):
        copy(ref, ref, out_sem.at[0], sem, at_x(x_peers[0])).wait_recv()

    def sent(ref, kind):
        copy(ref, ref, out_sem.at[kind], one_sem.at[0], at_x(x_peers[0])).wait_send()

    few, many = pl.ds(0, NX - 1), pl.ds(0, NZ - 1)
    own = r * NX + x

    for n, j in enumerate(x_peers + [x]):
        at = lanes(j)
        decay = mm(decay3, spread_marks(j), TN)
        decay_ref[:, at] = decay
        scaled = (decay * v_ref[:, at].astype(F32)).astype(BF16)
        scaled_ref[:, at] = scaled
        keep(0, j, mm(b, scaled, TN))
        if n == 0:
            pl.semaphore_wait(barrier, len(met))
            for i in x_peers:
                xd_copy(i).start()
        if n < NX - 1:
            x_copy(0, 0, j).start()
    for m in range(1, PIECES):
        for j in x_peers:
            x_copy(0, m, j).start()
    xdr_ref[x] = xd_ref[x]

    cum = thirds(mm(log3, 1.0 - later_b, NN))
    cum_ref[...] = cum
    marks_b = marks_f.astype(BF16)
    marks3 = jnp.concatenate([marks_b, marks_b, marks_b], axis=0)
    grow_ref[...] = mm(jnp.concatenate(split3(jnp.exp(cum)), axis=0), marks3, TN)
    for f in fetch[4:]:
        f.wait()
    c = c_ref[...]
    for n, j in enumerate(x_peers + [x]):
        at = lanes(j)
        gate = g_ref[:, at].astype(F32)
        sig = 1.0 / (1.0 + jnp.exp(-gate))
        out = go_ref[:, at].astype(F32)
        gy = out * (gate * sig)
        gy_ref[:, at] = gy
        gyb_ref[:, at] = gy.astype(BF16)
        gfac_ref[:, at] = out * sig * (1.0 + gate * (1.0 - sig))
        hi, lo = split2(grow_ref[:, at] * gy)
        gihi_ref[:, at] = hi
        gilo_ref[:, at] = lo
        keep(1, j, mm(c, hi, TN) + mm(c, lo, TN))
        if n < NX - 1:
            x_copy(1, 0, j).start()
        skipsum_ref[:, at] = jnp.sum(gy * v_ref[:, at].astype(F32), axis=0, keepdims=True)
    for m in range(1, PIECES):
        for j in x_peers:
            x_copy(1, m, j).start()
    for d in range(2):
        for m in range(PIECES):
            xr_ref[d, m, x] = xs_ref[d, m, x]

    got(xdr_ref.at[few], one_sem.at[0])
    for d in range(2):
        through = jnp.ones((1, SL), F32)
        for i in range(NX) if d == 0 else range(NX - 1, -1, -1):
            cs_ref[d, i] = through
            through = through * xdr_ref[i]
        if d == 0:
            zd_ref[...] = through
    zdr_ref[z] = zd_ref[...]
    for i in z_peers:
        zd_copy(i).start()

    def pair(p, carried):
        at = pl.ds(pl.multiple_of(p * 128, 128), 128)
        vp, gp = v_ref[:, at], gyb_ref[:, at]
        lane = iota((TOK, 128), 1)
        causal = iota((128, 128), 0) >= iota((128, 128), 1)
        intra = jnp.zeros((TOK, 128), F32)
        inner = jnp.zeros((TOK, 128), F32)
        for k in range(2):
            h = p * 2 + k
            own = jnp.where(lane < HEAD, 1.0 - k, float(k)).astype(BF16)
            vm, gm = vp * own, gp * own
            col = cumcol_ref[:, pl.ds(pl.multiple_of(h * 128, 128), 128)]
            row = cum_ref[pl.ds(h, 1), :]
            d00 = jnp.where(causal, jnp.exp(col[:128] - row[:, :128]), 0.0)
            d10 = jnp.exp(col[128:] - row[:, :128])
            d11 = jnp.where(causal, jnp.exp(col[128:] - row[:, 128:]), 0.0)
            grad = mm(gm, vp, NT)
            gsc_ref[:128, :128] += grad[:128, :128] * d00
            gsc_ref[128:, :128] += grad[128:, :128] * d10
            gsc_ref[128:, 128:] += grad[128:, 128:] * d11
            m00 = (sc_ref[:128, :128] * d00).astype(BF16)
            m10 = (sc_ref[128:, :128] * d10).astype(BF16)
            m11 = (sc_ref[128:, 128:] * d11).astype(BF16)
            mix = jnp.concatenate(
                [jnp.concatenate([m00, jnp.zeros_like(m00)], axis=1), jnp.concatenate([m10, m11], axis=1)], axis=0
            )
            intra = intra + mm(mix, vm, NN)
            inner = inner + mm(mix, gm, TN)
        intra_ref[:, at] = intra
        inner_ref[:, at] = inner
        w_ref[:, at] = gp.astype(F32) * intra - vp.astype(F32) * inner
        return carried

    def pairs(first, last):
        lax.fori_loop(first, last, pair, 0)

    def tile(i):
        return slice(i % 4 * 8, i % 4 * 8 + 8), slice(i // 4 * 128, i // 4 * 128 + 128)

    mine = pl.ds(pl.multiple_of(z // 4 * 128, 128), 128)

    def x_level(d, m):
        got(xr_ref.at[d, m, few], xr_sem.at[d, m])
        state = jnp.zeros((CR, SL), F32)
        for i in range(NX) if d == 0 else range(NX - 1, -1, -1):
            pre_ref[d, m, i] = state
            state = xdr_ref[i] * state + xr_ref[d, m, i]
        for i in range(NZ):
            zs_ref[d, m, i] = state[tile(i)]
        for i in z_peers:
            z_copy(d, m, i).start()
        zr_ref[d, m, z] = zs_ref[d, m, z]

    def z_level(d, m):
        got(zr_ref.at[d, m, many], zr_sem.at[d, m])
        state = jnp.zeros((8, 128), F32)
        for i in range(NZ) if d == 0 else range(NZ - 1, -1, -1):
            es_ref[d, m, i] = state
            state = zdr_ref[i, :, mine] * state + zr_ref[d, m, i]
        for i in z_peers:
            e_copy(d, m, i).start()
        er_ref[d, m, z] = es_ref[d, m, z]

    def back(d, m):
        got(er_ref.at[d, m, many], er_sem.at[d, m])
        for n, j in enumerate(x_peers + [x]):
            through = cs_ref[d, j]
            for i in range(NZ):
                rows, cols = tile(i)
                bs_ref[d, m, j, rows, cols] = pre_ref[d, m, j, rows, cols] + through[:, cols] * er_ref[d, m, i]
            if n < NX - 1:
                b_copy(d, m, j).start()
        br_ref[d, x, m * CR : (m + 1) * CR, :] = bs_ref[d, m, x]

    def arrived(d, m):
        got(br_ref.at[d, 0, pl.ds(0, (NX - 1) * CR)], br_sem.at[d, m])

    x_level(0, 0)

    sc_ref[...] = mm(c, b, NT)
    gsc_ref[...] = jnp.zeros_like(gsc_ref)
    cum3 = jnp.concatenate(split3(cum), axis=0)
    wide = jnp.where(head_rows(HEADS, 128), 1.0, 0.0).astype(BF16)
    cumcol_ref[...] = mm(cum3, jnp.concatenate([wide] * 3, axis=0), TN)
    x_level(0, 1)
    cumw_ref[...] = mm(cum3, marks3, TN)
    tot_ref[...] = jnp.sum(marks_f * total, axis=0, keepdims=True)
    skip_ref[...] = jnp.sum(marks_f * column(sg_ref[...]), axis=0, keepdims=True)
    pairs(0, 1)
    x_level(0, 2)
    pairs(1, 3)
    x_level(0, 3)
    got(zdr_ref.at[many], one_sem.at[1])
    z_level(0, 0)
    pairs(3, 4)
    x_level(1, 0)
    z_level(0, 1)
    pairs(4, 5)
    x_level(1, 1)
    z_level(0, 2)
    pairs(5, 6)
    x_level(1, 2)
    z_level(0, 3)
    back(0, 0)
    x_level(1, 3)
    z_level(1, 0)
    back(0, 1)
    pairs(6, 7)
    z_level(1, 1)
    back(0, 2)
    pairs(7, 8)
    z_level(1, 2)
    back(0, 3)
    z_level(1, 3)
    gsc_hi, gsc_lo = split2(gsc_ref[...])
    part_c = mm(gsc_hi, b, NN) + mm(gsc_lo, b, NN)
    part_b = mm(c, gsc_hi, TN) + mm(c, gsc_lo, TN)

    def moments(j):
        at = slice(j * SL, (j + 1) * SL)
        exact = decay_ref[:, at] * v_ref[:, at].astype(F32)
        for dst, what in ((sta_ref, exact), (mom_ref, exact * cumw_ref[:, at])):
            p0, p1, p2 = split3(what)
            dst[:, at] = mm(b, p0, TN) + mm(b, p1, TN) + mm(b, p2, TN)

    back(1, 0)
    moments(0)
    moments(1)
    back(1, 1)
    moments(2)
    moments(3)
    back(1, 2)
    back(1, 3)

    for m in range(PIECES):
        arrived(0, m)
    for j in range(NX):
        at = slice(j * SL, (j + 1) * SL)
        enter = br_ref[0, j]
        hi, lo = split2(enter)
        inter = mm(c, hi, NN) + mm(c, lo, NN)
        mamba = intra_ref[:, at] + grow_ref[:, at] * inter + skip_ref[:, at] * v_ref[:, at].astype(F32)
        gg_ref[:, at] = (gfac_ref[:, at] * mamba).astype(BF16)
        gi_hi, gi_lo = gihi_ref[:, at], gilo_ref[:, at]
        w = w_ref[:, at] + (gi_hi.astype(F32) + gi_lo.astype(F32)) * inter
        w_ref[:, at] = w
        rsum_ref[:, at] = jnp.sum(w * cumw_ref[:, at], axis=0, keepdims=True)
        mom_ref[:, at] = tot_ref[:, at] * (sta_ref[:, at] + dw_ref[:, at] * enter) - mom_ref[:, at]
        part_c = part_c + (mm(gi_hi, hi, NT) + mm(gi_lo, hi, NT) + mm(gi_hi, lo, NT))
    for q in range(NY):
        ysum_ref[q] = part_c[q * QT : (q + 1) * QT]
    for q in y_peers:
        ys_copy(q).start()
    yr_ref[y] = ysum_ref[y]

    def piece_b(m):
        rows = slice(m * CR, (m + 1) * CR)
        both = jnp.zeros((2 * CR, TOK), F32)
        for j in range(NX):
            pair_b = jnp.concatenate(split2(br_ref[1, j, rows, :]), axis=0)
            both = both + mm(pair_b, scaled_ref[:, j * SL : (j + 1) * SL], NT)
        hs_ref[m] = part_b[rows] + (both[:CR] + both[CR:])
        for q in y_peers:
            h_copy(m, q).start()
        hr_ref[m, y] = hs_ref[m]

    for m in range(PIECES - 1):
        arrived(1, m)
        piece_b(m)
    arrived(1, PIECES - 1)
    for j in range(NX):
        at = slice(j * SL, (j + 1) * SL)
        rsum_ref[:, at] += jnp.sum(br_ref[1, j] * mom_ref[:, at], axis=0, keepdims=True)

    rate_part = jnp.sum(jnp.where(marks, rsum_ref[...], 0.0), axis=1, keepdims=True)
    skip_part = jnp.sum(jnp.where(marks, skipsum_ref[...], 0.0), axis=1, keepdims=True)
    same = iota((HEADS, 128), 0) == iota((HEADS, 128), 1)
    rate_row = jnp.sum(jnp.where(same, rate_part, 0.0), axis=0, keepdims=True)
    skip_row = jnp.sum(jnp.where(same, skip_part, 0.0), axis=0, keepdims=True)
    m1s_ref[...] = jnp.where(iota((8, 128), 0) == 0, rate_row, skip_row)
    near = [(r, p) for p in x_peers] + [(other, p) for p in x_peers + [x]]
    for rr, p in near:
        m1_copy(rr, p).start()
    m1_ref[own] = m1s_ref[...]
    piece_b(PIECES - 1)

    for j in range(NX):
        at = slice(j * SL, (j + 1) * SL)
        after = br_ref[1, j]
        hi, lo = split2(after)
        grad_scaled = mm(b, hi, NN) + mm(b, lo, NN)
        out_decay = decay_ref[:, at]
        gv_ref[:, at] = (inner_ref[:, at] + out_decay * grad_scaled + skip_ref[:, at] * gy_ref[:, at]).astype(BF16)
        from_scaled = grad_scaled * (out_decay * v_ref[:, at].astype(F32))
        last = jnp.sum(from_scaled, axis=0, keepdims=True)
        last = last + dw_ref[:, at] * jnp.sum(after * br_ref[0, j], axis=0, keepdims=True)
        w_ref[:, at] = w_ref[:, at] - from_scaled
        w_ref[TOK - 1 : TOK, at] += last
    got(yr_ref.at[few], one_sem.at[2])
    ya_ref[...] = (yr_ref[0] + yr_ref[1]) + (yr_ref[2] + yr_ref[3])
    for q in y_peers:
        ya_copy(q).start()
    yg_ref[y] = ya_ref[...]
    got(m1_ref.at[pl.ds(0, NX * NR - 1)], one_sem.at[4])
    m2s_ref[...] = ((m1_ref[0] + m1_ref[1]) + (m1_ref[2] + m1_ref[3])) + ((m1_ref[4] + m1_ref[5]) + (m1_ref[6] + m1_ref[7]))
    for i in z_peers:
        m2_copy(i).start()
    m2_ref[z] = m2s_ref[...]
    grad_cum = jnp.zeros((HEADS, TOK), F32)
    for j in range(NX):
        at = slice(j * SL, (j + 1) * SL)
        mark = marks_b[:, at]
        w_hi, w_mid, w_lo = split3(w_ref[:, at])
        grad_cum = grad_cum + (mm(mark, w_hi, NT) + mm(mark, w_mid, NT) + mm(mark, w_lo, NT))
    gs_ref[...] = -rate * lanes_cumsum(grad_cum, True)
    for m in range(PIECES):
        got(hr_ref.at[m, few], hr_sem.at[m])
    gb_ref[...] = jnp.concatenate(
        [(hr_ref[m, 0] + hr_ref[m, 1]) + (hr_ref[m, 2] + hr_ref[m, 3]) for m in range(PIECES)], axis=0
    ).T
    got(yg_ref.at[few], one_sem.at[3])
    for q in range(NY):
        gc_ref[q * QT : (q + 1) * QT, :] = yg_ref[q]
    got(m2_ref.at[many], one_sem.at[5])
    sums = ((m2_ref[0] + m2_ref[1]) + (m2_ref[2] + m2_ref[3])) + ((m2_ref[4] + m2_ref[5]) + (m2_ref[6] + m2_ref[7]))
    rate_ref[...] = sums[0:1, 0:HEADS]
    skp_ref[...] = sums[1:2, 0:HEADS]

    sent(xs_ref.at[:, :, few], 0)
    sent(bs_ref.at[:, :, few], 1)
    sent(zs_ref.at[:, :, many], 2)
    sent(es_ref.at[:, :, many], 3)
    sent(xd_ref.at[few], 4)
    sent(zdr_ref.at[many], 5)
    sent(ysum_ref.at[few], 6)
    sent(yg_ref.at[few], 7)
    sent(hr_ref.at[:, few], 8)
    sent(m1_ref.at[pl.ds(0, NX * NR - 1)], 9)
    sent(m2_ref.at[many], 10)


def leave(*refs):
    count = len(refs) // 2
    moves = [pltpu.make_async_copy(refs[i], refs[count + i], refs[-1].at[i]) for i in range(count)]
    for move in moves:
        move.start()
    for move in moves:
        move.wait()


def block(values, gate_in, in_b, in_c, step_sizes, log_rates, skip_gain, grad_out):
    vmem = pl.BlockSpec(memory_space=pltpu.VMEM)
    anywhere = pl.BlockSpec(memory_space=pl.ANY)
    dma = pltpu.SemaphoreType.DMA
    wide, state = (TOK, WIDE), (TOK, STATE)
    scratch = [
        (wide, BF16), (wide, BF16), (state, BF16), (state, BF16), ((HEADS, TOK), F32), ((1, HEADS), F32), ((1, HEADS), F32),
        (wide, BF16),
        ((HEADS, TOK), F32), ((TOK, HEADS * 128), F32), (wide, F32), (wide, F32), ((1, WIDE), F32),
        (wide, BF16), (wide, F32), (wide, BF16), (wide, BF16), (wide, BF16),
        (wide, F32), ((TOK, TOK), F32), ((TOK, TOK), F32), (wide, F32), (wide, F32),
        (wide, F32), ((1, WIDE), F32), ((1, WIDE), F32), (wide, F32), ((1, WIDE), F32), ((1, WIDE), F32), ((STATE, WIDE), F32),
        ((STATE, WIDE), F32),
        ((NX, 1, SL), F32), ((NX, 1, SL), F32), ((2, NX, 1, SL), F32), ((1, SL), F32), ((NZ, 1, SL), F32),
        ((2, PIECES, NX, CR, SL), F32), ((2, PIECES, NX, CR, SL), F32), ((2, PIECES, NX, CR, SL), F32),
        ((2, PIECES, NZ, 8, 128), F32), ((2, PIECES, NZ, 8, 128), F32), ((2, PIECES, NZ, 8, 128), F32),
        ((2, PIECES, NZ, 8, 128), F32),
        ((2, PIECES, NX, CR, SL), F32), ((2, NX, STATE, SL), F32),
        ((NY, QT, STATE), F32), ((NY, QT, STATE), F32), ((QT, STATE), F32), ((NY, QT, STATE), F32),
        ((PIECES, CR, TOK), F32), ((PIECES, NY, CR, TOK), F32),
        ((8, 128), F32), ((NX * NR, 8, 128), F32), ((8, 128), F32), ((NZ, 8, 128), F32),
    ]
    sems = [(8,), (11,), (6,)] + [(2, PIECES)] * 4 + [(PIECES,)]
    outs = [(wide, BF16), (wide, BF16), (state, F32), (state, F32), ((HEADS, TOK), F32)] + [((1, HEADS), F32)] * 2
    held = pl.pallas_call(
        kernel,
        out_shape=[pltpu.VMEM(s, d) for s, d in outs],
        in_specs=[anywhere] * 8,
        out_specs=[vmem] * len(outs),
        scratch_shapes=[pltpu.VMEM(s, d) for s, d in scratch] + [dma(s) for s in sems],
        compiler_params=pltpu.CompilerParams(collective_id=0, has_side_effects=True),
    )(values[0], gate_in[0], in_b[0], in_c[0], step_sizes[0], log_rates[None], skip_gain[None], grad_out[0])
    gv, gg, gb, gc, gs, rates, skips = pl.pallas_call(
        leave,
        out_shape=[jax.ShapeDtypeStruct(s, d) for s, d in outs],
        in_specs=[anywhere] * len(outs),
        out_specs=[anywhere] * len(outs),
        scratch_shapes=[dma((len(outs),))],
        compiler_params=pltpu.CompilerParams(vmem_limit_bytes=1 << 20),
    )(*held)
    return gv[None], gg[None], gb[None], gc[None], gs[None], rates[0], skips[0]


def solution(mesh):
    wide = P("replica", "seq", "tensor")
    state = P("replica", "seq", None)
    step = P("replica", "tensor", "seq")
    head = P("tensor")
    return jax.shard_map(
        block,
        mesh=mesh,
        in_specs=(wide, wide, state, state, step, head, head, wide),
        out_specs=(wide, wide, state, state, step, head, head),
        check_vma=False,
    )
```

```python
import jax
import jax.numpy as jnp
from jax import lax
from jax.experimental import pallas as pl
from jax.experimental.pallas import tpu as pltpu
from jax.sharding import PartitionSpec as P

F32 = jnp.float32
BF16 = jnp.bfloat16
NX, NZ, NY, NR = 4, 8, 4, 2
HEADS, HEAD, STATE, TOK = 16, 64, 128, 256
WIDE = HEADS * HEAD
SL = WIDE // NX
PIECES = 4
CR = STATE // PIECES
QT = TOK // NY
NT = (((1,), (1,)), ((), ()))
TN = (((0,), (0,)), ((), ()))
NN = (((1,), (0,)), ((), ()))


def mm(a, b, dims):
    return lax.dot_general(a, b, dims, preferred_element_type=F32)


def split2(x):
    hi = x.astype(BF16)
    return hi, (x - hi.astype(F32)).astype(BF16)


def split3(x):
    hi = x.astype(BF16)
    rest = x - hi.astype(F32)
    mid = rest.astype(BF16)
    return hi, mid, (rest - mid.astype(F32)).astype(BF16)


def iota(shape, dim):
    return lax.broadcasted_iota(jnp.int32, shape, dim)


def column(row):
    n = row.shape[1]
    same = iota((n, n), 0) == iota((n, n), 1)
    return jnp.sum(jnp.where(same, jnp.broadcast_to(row, (n, n)), 0.0), axis=1, keepdims=True)


def lanes_cumsum(x, reverse):
    n = x.shape[1]
    lane = iota(x.shape, 1)
    by = 1
    while by < n:
        if reverse:
            x = x + jnp.where(lane < n - by, pltpu.roll(x, n - by, 1), 0.0)
        else:
            x = x + jnp.where(lane >= by, pltpu.roll(x, by, 1), 0.0)
        by *= 2
    return x


def head_rows(rows, width):
    shape = (rows, rows * width)
    start = iota(shape, 0) * width
    lane = iota(shape, 1)
    return (lane >= start) & (lane < start + width)


def kernel(
    v_hbm, g_hbm, b_hbm, c_hbm, st_hbm, lr_hbm, sg_hbm, go_hbm,
    gv_ref, gg_ref, gb_ref, gc_ref, gs_ref, rate_ref, skp_ref,
    v_ref, g_ref, b_ref, c_ref, st_ref, lr_ref, sg_ref, go_ref,
    cum_ref, cumcol_ref, grow_ref, decay_ref, skip_ref, scaled_ref, gy_ref, gyb_ref, gihi_ref, gilo_ref,
    gfac_ref, sc_ref, gsc_ref, intra_ref, inner_ref, w_ref, dw_ref, skipsum_ref, cumw_ref, tot_ref, rsum_ref, mom_ref, sta_ref,
    xd_ref, xdr_ref, cs_ref, zd_ref, zdr_ref,
    xs_ref, xr_ref, pre_ref, zs_ref, zr_ref, es_ref, er_ref, bs_ref, br_ref,
    ysum_ref, yr_ref, ya_ref, yg_ref, hs_ref, hr_ref, m1s_ref, m1_ref, m2s_ref, m2_ref,
    in_sem, out_sem, one_sem, xr_sem, zr_sem, er_sem, br_sem, hr_sem,
):
    r = lax.axis_index("replica")
    seq = lax.axis_index("seq")
    y = lax.axis_index("tensor")
    z, x = seq // NX, seq % NX

    fetch = [
        pltpu.make_async_copy(src, dst, in_sem.at[i])
        for i, (src, dst) in enumerate((
            (lr_hbm, lr_ref), (st_hbm, st_ref), (b_hbm, b_ref), (v_hbm, v_ref),
            (c_hbm, c_ref), (g_hbm, g_ref), (go_hbm, go_ref), (sg_hbm, sg_ref),
        ))
    ]
    for f in fetch:
        f.start()

    barrier = pltpu.get_barrier_semaphore()

    def at_x(to):
        return (r, z * NX + to, y)

    def at_z(to):
        return (r, to * NX + x, y)

    def at_y(to):
        return (r, seq, to)

    x_peers = [(x + o) % NX for o in (2, 1, 3)]
    z_peers = [(z + o) % NZ for o in (4, 3, 5, 2, 6, 1, 7)]
    y_peers = [(y + o) % NY for o in (2, 1, 3)]
    other = (r + 1) % NR
    met = [at_z(p) for p in z_peers] + [at_x(p) for p in x_peers] + [at_y(p) for p in y_peers]
    met += [(other, seq, y)]
    for device in met:
        pl.semaphore_signal(barrier, inc=1, device_id=device, device_id_type=pl.DeviceIdType.MESH)

    def copy(src, dst, s, d, device):
        return pltpu.make_async_remote_copy(
            src_ref=src, dst_ref=dst, send_sem=s, recv_sem=d,
            device_id=device, device_id_type=pl.DeviceIdType.MESH,
        )

    later = iota((TOK, TOK), 0) > iota((TOK, TOK), 1)
    later_b = jnp.where(later, 1.0, 0.0).astype(BF16)

    def thirds(p):
        return (p[:HEADS] + p[HEADS : 2 * HEADS]) + p[2 * HEADS :]

    def spread_marks(j):
        start = (iota((3 * HEADS, SL), 0) % HEADS) * HEAD - j * SL
        lane = iota((3 * HEADS, SL), 1)
        return jnp.where((lane >= start) & (lane < start + HEAD), 1.0, 0.0).astype(BF16)

    for f in fetch[:2]:
        f.wait()
    rate = jnp.exp(column(lr_ref[...]))
    steps = st_ref[...]
    log = -rate * steps
    log3 = jnp.concatenate(split3(log), axis=0)
    suffix = thirds(mm(log3, later_b, NN))
    decay3 = jnp.concatenate(split3(jnp.exp(suffix)), axis=0)
    total = suffix[:, 0:1] + log[:, 0:1]
    marks = head_rows(HEADS, HEAD)
    marks_f = jnp.where(marks, 1.0, 0.0)
    dw_ref[...] = jnp.sum(marks_f * jnp.exp(total), axis=0, keepdims=True)
    for j in range(NX):
        xd_ref[j] = dw_ref[:, j * SL : (j + 1) * SL]
    for f in fetch[2:4]:
        f.wait()
    b = b_ref[...]

    def lanes(j):
        return pl.ds(pl.multiple_of(j * SL, SL), SL)

    def keep(d, j, state):
        for m in range(PIECES):
            xs_ref[d, m, j] = state[m * CR : (m + 1) * CR]

    def x_copy(d, m, j):
        return copy(xs_ref.at[d, m, j], xr_ref.at[d, m, x], out_sem.at[0], xr_sem.at[d, m], at_x(j))

    def b_copy(d, m, j):
        return copy(bs_ref.at[d, m, j], br_ref.at[d, x, pl.ds(m * CR, CR)], out_sem.at[1], br_sem.at[d, m], at_x(j))

    def z_copy(d, m, j):
        return copy(zs_ref.at[d, m, j], zr_ref.at[d, m, z], out_sem.at[2], zr_sem.at[d, m], at_z(j))

    def e_copy(d, m, j):
        return copy(es_ref.at[d, m, j], er_ref.at[d, m, z], out_sem.at[3], er_sem.at[d, m], at_z(j))

    def xd_copy(j):
        return copy(xd_ref.at[j], xdr_ref.at[x], out_sem.at[4], one_sem.at[0], at_x(j))

    def zd_copy(j):
        return copy(zd_ref, zdr_ref.at[z], out_sem.at[5], one_sem.at[1], at_z(j))

    def ys_copy(j):
        return copy(ysum_ref.at[j], yr_ref.at[y], out_sem.at[6], one_sem.at[2], at_y(j))

    def ya_copy(j):
        return copy(ya_ref, yg_ref.at[y], out_sem.at[7], one_sem.at[3], at_y(j))

    def h_copy(m, j):
        return copy(hs_ref.at[m], hr_ref.at[m, y], out_sem.at[8], hr_sem.at[m], at_y(j))

    def m1_copy():
        return copy(m1s_ref, m1_ref.at[r], out_sem.at[9], one_sem.at[4], (other, seq, y))

    def m2_copy(j):
        return copy(m2s_ref, m2_ref.at[seq], out_sem.at[10], one_sem.at[5], (r, j, y))

    def got(ref, sem):
        copy(ref, ref, out_sem.at[0], sem, at_x(x_peers[0])).wait_recv()

    def sent(ref, kind):
        copy(ref, ref, out_sem.at[kind], one_sem.at[0], at_x(x_peers[0])).wait_send()

    few, many = pl.ds(0, NX - 1), pl.ds(0, NZ - 1)

    for n, j in enumerate(x_peers + [x]):
        at = lanes(j)
        decay = mm(decay3, spread_marks(j), TN)
        decay_ref[:, at] = decay
        scaled = (decay * v_ref[:, at].astype(F32)).astype(BF16)
        scaled_ref[:, at] = scaled
        keep(0, j, mm(b, scaled, TN))
        if n == 0:
            pl.semaphore_wait(barrier, len(met))
            for i in x_peers:
                xd_copy(i).start()
        if n < NX - 1:
            x_copy(0, 0, j).start()
    for m in range(1, PIECES):
        for j in x_peers:
            x_copy(0, m, j).start()
    xdr_ref[x] = xd_ref[x]

    cum = thirds(mm(log3, 1.0 - later_b, NN))
    cum_ref[...] = cum
    marks_b = marks_f.astype(BF16)
    marks3 = jnp.concatenate([marks_b, marks_b, marks_b], axis=0)
    grow_ref[...] = mm(jnp.concatenate(split3(jnp.exp(cum)), axis=0), marks3, TN)
    for f in fetch[4:]:
        f.wait()
    c = c_ref[...]
    for n, j in enumerate(x_peers + [x]):
        at = lanes(j)
        gate = g_ref[:, at].astype(F32)
        sig = 1.0 / (1.0 + jnp.exp(-gate))
        out = go_ref[:, at].astype(F32)
        gy = out * (gate * sig)
        gy_ref[:, at] = gy
        gyb_ref[:, at] = gy.astype(BF16)
        gfac_ref[:, at] = out * sig * (1.0 + gate * (1.0 - sig))
        hi, lo = split2(grow_ref[:, at] * gy)
        gihi_ref[:, at] = hi
        gilo_ref[:, at] = lo
        keep(1, j, mm(c, hi, TN) + mm(c, lo, TN))
        if n < NX - 1:
            x_copy(1, 0, j).start()
        skipsum_ref[:, at] = jnp.sum(gy * v_ref[:, at].astype(F32), axis=0, keepdims=True)
    for m in range(1, PIECES):
        for j in x_peers:
            x_copy(1, m, j).start()
    for d in range(2):
        for m in range(PIECES):
            xr_ref[d, m, x] = xs_ref[d, m, x]

    got(xdr_ref.at[few], one_sem.at[0])
    for d in range(2):
        through = jnp.ones((1, SL), F32)
        for i in range(NX) if d == 0 else range(NX - 1, -1, -1):
            cs_ref[d, i] = through
            through = through * xdr_ref[i]
        if d == 0:
            zd_ref[...] = through
    zdr_ref[z] = zd_ref[...]
    for i in z_peers:
        zd_copy(i).start()

    def pair(p, carried):
        at = pl.ds(pl.multiple_of(p * 128, 128), 128)
        vp, gp = v_ref[:, at], gyb_ref[:, at]
        lane = iota((TOK, 128), 1)
        causal = iota((128, 128), 0) >= iota((128, 128), 1)
        intra = jnp.zeros((TOK, 128), F32)
        inner = jnp.zeros((TOK, 128), F32)
        for k in range(2):
            h = p * 2 + k
            own = jnp.where(lane < HEAD, 1.0 - k, float(k)).astype(BF16)
            vm, gm = vp * own, gp * own
            col = cumcol_ref[:, pl.ds(pl.multiple_of(h * 128, 128), 128)]
            row = cum_ref[pl.ds(h, 1), :]
            d00 = jnp.where(causal, jnp.exp(col[:128] - row[:, :128]), 0.0)
            d10 = jnp.exp(col[128:] - row[:, :128])
            d11 = jnp.where(causal, jnp.exp(col[128:] - row[:, 128:]), 0.0)
            grad = mm(gm, vp, NT)
            gsc_ref[:128, :128] += grad[:128, :128] * d00
            gsc_ref[128:, :128] += grad[128:, :128] * d10
            gsc_ref[128:, 128:] += grad[128:, 128:] * d11
            m00 = (sc_ref[:128, :128] * d00).astype(BF16)
            m10 = (sc_ref[128:, :128] * d10).astype(BF16)
            m11 = (sc_ref[128:, 128:] * d11).astype(BF16)
            mix = jnp.concatenate(
                [jnp.concatenate([m00, jnp.zeros_like(m00)], axis=1), jnp.concatenate([m10, m11], axis=1)], axis=0
            )
            intra = intra + mm(mix, vm, NN)
            inner = inner + mm(mix, gm, TN)
        intra_ref[:, at] = intra
        inner_ref[:, at] = inner
        w_ref[:, at] = gp.astype(F32) * intra - vp.astype(F32) * inner
        return carried

    def pairs(first, last):
        lax.fori_loop(first, last, pair, 0)

    def tile(i):
        return slice(i % 4 * 8, i % 4 * 8 + 8), slice(i // 4 * 128, i // 4 * 128 + 128)

    mine = pl.ds(pl.multiple_of(z // 4 * 128, 128), 128)

    def x_level(d, m):
        got(xr_ref.at[d, m, few], xr_sem.at[d, m])
        state = jnp.zeros((CR, SL), F32)
        for i in range(NX) if d == 0 else range(NX - 1, -1, -1):
            pre_ref[d, m, i] = state
            state = xdr_ref[i] * state + xr_ref[d, m, i]
        for i in range(NZ):
            zs_ref[d, m, i] = state[tile(i)]
        for i in z_peers:
            z_copy(d, m, i).start()
        zr_ref[d, m, z] = zs_ref[d, m, z]

    def z_level(d, m):
        got(zr_ref.at[d, m, many], zr_sem.at[d, m])
        state = jnp.zeros((8, 128), F32)
        for i in range(NZ) if d == 0 else range(NZ - 1, -1, -1):
            es_ref[d, m, i] = state
            state = zdr_ref[i, :, mine] * state + zr_ref[d, m, i]
        for i in z_peers:
            e_copy(d, m, i).start()
        er_ref[d, m, z] = es_ref[d, m, z]

    def back(d, m):
        got(er_ref.at[d, m, many], er_sem.at[d, m])
        for n, j in enumerate(x_peers + [x]):
            through = cs_ref[d, j]
            for i in range(NZ):
                rows, cols = tile(i)
                bs_ref[d, m, j, rows, cols] = pre_ref[d, m, j, rows, cols] + through[:, cols] * er_ref[d, m, i]
            if n < NX - 1:
                b_copy(d, m, j).start()
        br_ref[d, x, m * CR : (m + 1) * CR, :] = bs_ref[d, m, x]

    def arrived(d, m):
        got(br_ref.at[d, 0, pl.ds(0, (NX - 1) * CR)], br_sem.at[d, m])

    x_level(0, 0)

    sc_ref[...] = mm(c, b, NT)
    gsc_ref[...] = jnp.zeros_like(gsc_ref)
    cum3 = jnp.concatenate(split3(cum), axis=0)
    wide = jnp.where(head_rows(HEADS, 128), 1.0, 0.0).astype(BF16)
    cumcol_ref[...] = mm(cum3, jnp.concatenate([wide] * 3, axis=0), TN)
    x_level(0, 1)
    cumw_ref[...] = mm(cum3, marks3, TN)
    tot_ref[...] = jnp.sum(marks_f * total, axis=0, keepdims=True)
    skip_ref[...] = jnp.sum(marks_f * column(sg_ref[...]), axis=0, keepdims=True)
    pairs(0, 1)
    x_level(0, 2)
    pairs(1, 3)
    x_level(0, 3)
    got(zdr_ref.at[many], one_sem.at[1])
    z_level(0, 0)
    pairs(3, 4)
    x_level(1, 0)
    z_level(0, 1)
    pairs(4, 5)
    x_level(1, 1)
    z_level(0, 2)
    pairs(5, 6)
    x_level(1, 2)
    z_level(0, 3)
    back(0, 0)
    x_level(1, 3)
    z_level(1, 0)
    back(0, 1)
    pairs(6, 7)
    z_level(1, 1)
    back(0, 2)
    pairs(7, 8)
    z_level(1, 2)
    back(0, 3)
    z_level(1, 3)
    gsc_hi, gsc_lo = split2(gsc_ref[...])
    part_c = mm(gsc_hi, b, NN) + mm(gsc_lo, b, NN)
    part_b = mm(c, gsc_hi, TN) + mm(c, gsc_lo, TN)

    def moments(j):
        at = slice(j * SL, (j + 1) * SL)
        exact = decay_ref[:, at] * v_ref[:, at].astype(F32)
        for dst, what in ((sta_ref, exact), (mom_ref, exact * cumw_ref[:, at])):
            p0, p1, p2 = split3(what)
            dst[:, at] = mm(b, p0, TN) + mm(b, p1, TN) + mm(b, p2, TN)

    back(1, 0)
    moments(0)
    moments(1)
    back(1, 1)
    moments(2)
    moments(3)
    back(1, 2)
    back(1, 3)

    for m in range(PIECES):
        arrived(0, m)
    for j in range(NX):
        at = slice(j * SL, (j + 1) * SL)
        enter = br_ref[0, j]
        hi, lo = split2(enter)
        inter = mm(c, hi, NN) + mm(c, lo, NN)
        mamba = intra_ref[:, at] + grow_ref[:, at] * inter + skip_ref[:, at] * v_ref[:, at].astype(F32)
        gg_ref[:, at] = (gfac_ref[:, at] * mamba).astype(BF16)
        gi_hi, gi_lo = gihi_ref[:, at], gilo_ref[:, at]
        w = w_ref[:, at] + (gi_hi.astype(F32) + gi_lo.astype(F32)) * inter
        w_ref[:, at] = w
        rsum_ref[:, at] = jnp.sum(w * cumw_ref[:, at], axis=0, keepdims=True)
        mom_ref[:, at] = tot_ref[:, at] * (sta_ref[:, at] + dw_ref[:, at] * enter) - mom_ref[:, at]
        part_c = part_c + (mm(gi_hi, hi, NT) + mm(gi_lo, hi, NT) + mm(gi_hi, lo, NT))
    for q in range(NY):
        ysum_ref[q] = part_c[q * QT : (q + 1) * QT]
    for q in y_peers:
        ys_copy(q).start()
    yr_ref[y] = ysum_ref[y]

    def piece_b(m):
        rows = slice(m * CR, (m + 1) * CR)
        both = jnp.zeros((2 * CR, TOK), F32)
        for j in range(NX):
            pair_b = jnp.concatenate(split2(br_ref[1, j, rows, :]), axis=0)
            both = both + mm(pair_b, scaled_ref[:, j * SL : (j + 1) * SL], NT)
        hs_ref[m] = part_b[rows] + (both[:CR] + both[CR:])
        for q in y_peers:
            h_copy(m, q).start()
        hr_ref[m, y] = hs_ref[m]

    for m in range(PIECES - 1):
        arrived(1, m)
        piece_b(m)
    arrived(1, PIECES - 1)
    for j in range(NX):
        at = slice(j * SL, (j + 1) * SL)
        rsum_ref[:, at] += jnp.sum(br_ref[1, j] * mom_ref[:, at], axis=0, keepdims=True)

    rate_part = jnp.sum(jnp.where(marks, rsum_ref[...], 0.0), axis=1, keepdims=True)
    skip_part = jnp.sum(jnp.where(marks, skipsum_ref[...], 0.0), axis=1, keepdims=True)
    row, lane = iota((HEADS, 128), 0), iota((HEADS, 128), 1)
    packed = jnp.where(lane == row, rate_part, jnp.where(lane == row + HEADS, skip_part, 0.0))
    m1s_ref[...] = jnp.sum(packed, axis=0, keepdims=True)
    m1_copy().start()
    m1_ref[r] = m1s_ref[...]
    piece_b(PIECES - 1)
    got(m1_ref.at[pl.ds(0, 1)], one_sem.at[4])
    m2s_ref[...] = m1_ref[0] + m1_ref[1]
    for oz in (4, 3, 5, 2, 6, 1, 7, 0):
        for ox in (2, 1, 3, 0):
            if (oz, ox) != (0, 0):
                m2_copy((z + oz) % NZ * NX + (x + ox) % NX).start()
    m2_ref[seq] = m2s_ref[...]
    got(yr_ref.at[few], one_sem.at[2])
    ya_ref[...] = (yr_ref[0] + yr_ref[1]) + (yr_ref[2] + yr_ref[3])
    for q in y_peers:
        ya_copy(q).start()
    yg_ref[y] = ya_ref[...]

    for j in range(NX):
        at = slice(j * SL, (j + 1) * SL)
        after = br_ref[1, j]
        hi, lo = split2(after)
        grad_scaled = mm(b, hi, NN) + mm(b, lo, NN)
        out_decay = decay_ref[:, at]
        gv_ref[:, at] = (inner_ref[:, at] + out_decay * grad_scaled + skip_ref[:, at] * gy_ref[:, at]).astype(BF16)
        from_scaled = grad_scaled * (out_decay * v_ref[:, at].astype(F32))
        last = jnp.sum(from_scaled, axis=0, keepdims=True)
        last = last + dw_ref[:, at] * jnp.sum(after * br_ref[0, j], axis=0, keepdims=True)
        w_ref[:, at] = w_ref[:, at] - from_scaled
        w_ref[TOK - 1 : TOK, at] += last
    grad_cum = jnp.zeros((HEADS, TOK), F32)
    for j in range(NX):
        at = slice(j * SL, (j + 1) * SL)
        mark = marks_b[:, at]
        w_hi, w_mid, w_lo = split3(w_ref[:, at])
        grad_cum = grad_cum + (mm(mark, w_hi, NT) + mm(mark, w_mid, NT) + mm(mark, w_lo, NT))
    gs_ref[...] = -rate * lanes_cumsum(grad_cum, True)
    for m in range(PIECES):
        got(hr_ref.at[m, few], hr_sem.at[m])
    gb_ref[...] = jnp.concatenate(
        [(hr_ref[m, 0] + hr_ref[m, 1]) + (hr_ref[m, 2] + hr_ref[m, 3]) for m in range(PIECES)], axis=0
    ).T
    got(yg_ref.at[few], one_sem.at[3])
    for q in range(NY):
        gc_ref[q * QT : (q + 1) * QT, :] = yg_ref[q]
    got(m2_ref.at[pl.ds(0, NX * NZ - 1)], one_sem.at[5])
    sums = [m2_ref[i] for i in range(NX * NZ)]
    while len(sums) > 1:
        sums = [u + v for u, v in zip(sums[0::2], sums[1::2])]
    rate_ref[...] = sums[0][:, 0:HEADS]
    skp_ref[...] = sums[0][:, HEADS : 2 * HEADS]

    sent(xs_ref.at[:, :, few], 0)
    sent(bs_ref.at[:, :, few], 1)
    sent(zs_ref.at[:, :, many], 2)
    sent(es_ref.at[:, :, many], 3)
    sent(xd_ref.at[few], 4)
    sent(zdr_ref.at[many], 5)
    sent(ysum_ref.at[few], 6)
    sent(yg_ref.at[few], 7)
    sent(hr_ref.at[:, few], 8)
    sent(m1_ref.at[pl.ds(0, 1)], 9)
    sent(m2_ref.at[pl.ds(0, NX * NZ - 1)], 10)


def leave(*refs):
    count = len(refs) // 2
    moves = [pltpu.make_async_copy(refs[i], refs[count + i], refs[-1].at[i]) for i in range(count)]
    for move in moves:
        move.start()
    for move in moves:
        move.wait()


def block(values, gate_in, in_b, in_c, step_sizes, log_rates, skip_gain, grad_out):
    vmem = pl.BlockSpec(memory_space=pltpu.VMEM)
    anywhere = pl.BlockSpec(memory_space=pl.ANY)
    dma = pltpu.SemaphoreType.DMA
    wide, state = (TOK, WIDE), (TOK, STATE)
    scratch = [
        (wide, BF16), (wide, BF16), (state, BF16), (state, BF16), ((HEADS, TOK), F32), ((1, HEADS), F32), ((1, HEADS), F32),
        (wide, BF16),
        ((HEADS, TOK), F32), ((TOK, HEADS * 128), F32), (wide, F32), (wide, F32), ((1, WIDE), F32),
        (wide, BF16), (wide, F32), (wide, BF16), (wide, BF16), (wide, BF16),
        (wide, F32), ((TOK, TOK), F32), ((TOK, TOK), F32), (wide, F32), (wide, F32),
        (wide, F32), ((1, WIDE), F32), ((1, WIDE), F32), (wide, F32), ((1, WIDE), F32), ((1, WIDE), F32), ((STATE, WIDE), F32),
        ((STATE, WIDE), F32),
        ((NX, 1, SL), F32), ((NX, 1, SL), F32), ((2, NX, 1, SL), F32), ((1, SL), F32), ((NZ, 1, SL), F32),
        ((2, PIECES, NX, CR, SL), F32), ((2, PIECES, NX, CR, SL), F32), ((2, PIECES, NX, CR, SL), F32),
        ((2, PIECES, NZ, 8, 128), F32), ((2, PIECES, NZ, 8, 128), F32), ((2, PIECES, NZ, 8, 128), F32),
        ((2, PIECES, NZ, 8, 128), F32),
        ((2, PIECES, NX, CR, SL), F32), ((2, NX, STATE, SL), F32),
        ((NY, QT, STATE), F32), ((NY, QT, STATE), F32), ((QT, STATE), F32), ((NY, QT, STATE), F32),
        ((PIECES, CR, TOK), F32), ((PIECES, NY, CR, TOK), F32),
        ((1, 128), F32), ((NR, 1, 128), F32), ((1, 128), F32), ((NX * NZ, 1, 128), F32),
    ]
    sems = [(8,), (11,), (6,)] + [(2, PIECES)] * 4 + [(PIECES,)]
    outs = [(wide, BF16), (wide, BF16), (state, F32), (state, F32), ((HEADS, TOK), F32)] + [((1, HEADS), F32)] * 2
    held = pl.pallas_call(
        kernel,
        out_shape=[pltpu.VMEM(s, d) for s, d in outs],
        in_specs=[anywhere] * 8,
        out_specs=[vmem] * len(outs),
        scratch_shapes=[pltpu.VMEM(s, d) for s, d in scratch] + [dma(s) for s in sems],
        compiler_params=pltpu.CompilerParams(collective_id=0, has_side_effects=True),
    )(values[0], gate_in[0], in_b[0], in_c[0], step_sizes[0], log_rates[None], skip_gain[None], grad_out[0])
    gv, gg, gb, gc, gs, rates, skips = pl.pallas_call(
        leave,
        out_shape=[jax.ShapeDtypeStruct(s, d) for s, d in outs],
        in_specs=[anywhere] * len(outs),
        out_specs=[anywhere] * len(outs),
        scratch_shapes=[dma((len(outs),))],
        compiler_params=pltpu.CompilerParams(vmem_limit_bytes=1 << 20),
    )(*held)
    return gv[None], gg[None], gb[None], gc[None], gs[None], rates[0], skips[0]


def solution(mesh):
    wide = P("replica", "seq", "tensor")
    state = P("replica", "seq", None)
    step = P("replica", "tensor", "seq")
    head = P("tensor")
    return jax.shard_map(
        block,
        mesh=mesh,
        in_specs=(wide, wide, state, state, step, head, head, wide),
        out_specs=(wide, wide, state, state, step, head, head),
        check_vma=False,
    )
```
